256 devices in a mesh: src: 16 (over z_lo, y), tgt: 16 (over x, z_hi, core).
Axes of the slice: x: 4, y: 4, z: 8 (z_hi: 2, z_lo: 4; z = z_hi * 4 + z_lo), core: 2. Of those that a mesh axis runs over, the one named last changes fastest.
Arguments:
- coefficients: bfloat16 [65536, 16, 128], P(('src', 'tgt')), may hold values from -6 to 6
- phases: float32 [8, 65536, 64], P(None, ('src', 'tgt')), may hold values from -3.140625 to 3.140625
- classes: int32 [8, 65536], P(None, ('src', 'tgt')), may hold values from 0 to 1
- blocks: bfloat16 [8, 2, 2, 128, 256], replicated, may hold values from -0.375 to 0.375
- evaluation: bfloat16 [128, 128], replicated, may hold values from -0.125 to 0.125
Outputs:
- target_values: bfloat16 [16, 256, 16, 128], P('tgt', 'src')
The draws below stay inside these ranges and needn't reach their ends.
All inputs are finite; a program needn't handle non-finite values.
Results may differ from the reference program's by a relative error of at most 0.029.
Values may be sent and summed in bfloat16 or wider, within the bound.
A program may use at most 64 MiB of HBM per device.

```python
import jax
import jax.numpy as jnp
from jax import lax

RANK = 64
RHS = 16
LEVELS = 8
CLASSES = 2
NB_DEV = 256
NBTOT = 65536
N_SRC = 16
N_TGT = 16


def set_ends(drawn, own_key, least, high):
    dims = drawn.shape
    index_at = [jax.random.randint(jax.random.fold_in(own_key, axis), (), 0, dims[axis]) for axis in range(len(dims))]
    drawn = drawn.at[tuple(index_at)].set(least)
    longest = dims.index(max(dims))
    index_at[longest] = (index_at[longest] + 1) % dims[longest]
    return drawn.at[tuple(index_at)].set(high)


def levels(rng, extent, shards, least, largest):
    level = 1.0
    for position, shards_of in shards:
        draws = jax.random.uniform(jax.random.fold_in(jax.random.fold_in(rng, 6), position), (shards_of,), jnp.float32, least / len(shards), largest / len(shards))
        level = level * jnp.repeat(jnp.exp(draws), extent[position] // shards_of).reshape((-1,) + (1,) * (len(extent) - 1 - position))
    return level


def bell_draw(stream_key, extent, scale, reach, split=(), kind=jnp.bfloat16):
    drawn = jax.random.normal(stream_key, extent, jnp.float32) * scale
    if len(split) > 0:
        drawn = levels(stream_key, extent, split, -0.22, 0.18) * drawn
    return jnp.clip(drawn, min=-reach, max=reach).astype(kind)


def setup_inputs(seed: int = 0) -> dict:
    seeds = jax.random.split(jax.random.key(seed), 6)
    return {
        "coefficients": bell_draw(seeds[0], (NBTOT, RHS, 2 * RANK), 1.0, 6.0, ((0, 256),)),
        "phases": jnp.clip(jax.random.uniform(seeds[1], (LEVELS, NBTOT, RANK), jnp.float32, -3.140625, 3.140625), -3.140625, 3.140625),
        "classes": set_ends(jax.random.randint(seeds[2], (LEVELS, NBTOT), 0, CLASSES), jax.random.fold_in(seeds[2], 1), 0, CLASSES - 1).astype(jnp.int32),
        "blocks": bell_draw(seeds[3], (LEVELS, CLASSES, 2, 2 * RANK, 4 * RANK), (4 * RANK) ** -0.5, 0.375),
        "evaluation": bell_draw(seeds[4], (2 * RANK, 2 * RANK), (2 * RANK * N_SRC) ** -0.5, 0.125),
    }


def rotate_phase(values, angles):
    half = angles.shape[-1]
    cosine = jnp.cos(angles)[..., None, :]
    sine = jnp.sin(angles)[..., None, :]
    real_part = values[..., :half]
    imag_part = values[..., half:]
    return jnp.concatenate([cosine * real_part - sine * imag_part, sine * real_part + cosine * imag_part], axis=-1)


def reference(coefficients, phases, classes, blocks, evaluation):
    current = coefficients
    total = current.shape[0]
    rhs_count = current.shape[1]
    width = current.shape[2]
    for level in range(LEVELS):
        if level % 2 == 0:
            nbits = int(N_SRC).bit_length() - 1
            stride = NB_DEV * N_TGT * 2 ** ((level // 2) % nbits)
        else:
            nbits = int(N_TGT).bit_length() - 1
            stride = NB_DEV * 2 ** ((level // 2) % nbits)
        groups = total // (2 * stride)
        split_state = current.reshape(groups, 2, stride, rhs_count, width).astype(jnp.float32)
        split_classes = classes[level].reshape(groups, 2, stride)
        split_angles = phases[level].reshape(groups, 2, stride, width // 2)
        parts = []
        for child in range(2):
            accumulated = jnp.zeros((groups, stride, rhs_count, 2 * width), jnp.float32)
            for which in range(CLASSES):
                product = jnp.einsum("hskc,cd->hskd", split_state[:, child], blocks[level, which, child].astype(jnp.float32), precision=lax.Precision.HIGHEST)
                accumulated = accumulated + jnp.where((split_classes[:, child] == which)[:, :, None, None], product, 0.0)
            parts.append(accumulated)
        outputs = []
        for child in range(2):
            summed = parts[0][..., child * width:(child + 1) * width] + parts[1][..., child * width:(child + 1) * width]
            outputs.append(rotate_phase(summed, split_angles[:, child]))
        current = jnp.stack(outputs, axis=1).reshape(total, rhs_count, width).astype(jnp.bfloat16)
    final_state = current.reshape(N_SRC, N_TGT, NB_DEV, rhs_count, width).astype(jnp.float32)
    result = jnp.einsum("stnkc,cd->tnkd", final_state, evaluation.astype(jnp.float32), precision=lax.Precision.HIGHEST)
    return result.astype(jnp.bfloat16)
```

```python
import jax
import jax.numpy as jnp
from jax import lax
from jax.experimental import pallas as pl
from jax.experimental.pallas import tpu as pltpu
from jax.sharding import PartitionSpec as P

MESH = pl.DeviceIdType.MESH
SIN = (3.1415927410125732, -5.167712688446045, 2.5501604080200195, -0.5992423295974731,
       0.08208189159631729, -0.007275315932929516, 0.0003952804545406252)
COS = (1.0, -4.93480110168457, 4.058694839477539, -1.3351584672927856,
       0.23502980172634125, -0.025358984246850014, 0.0015939107397571206)
STEP = 10430.378350470453


def horner(coefs, v):
    acc = jnp.full_like(v, coefs[-1])
    for a in coefs[-2::-1]:
        acc = acc * v + a
    return acc


def sin_cos(k):
    u = k.astype(jnp.float32) * (1.0 / 32768.0)
    v = u * u
    return u * horner(SIN, v), horner(COS, v)


def high(w):
    return w >> 16


def low(w):
    return (w << 16) >> 16


def word(a, b):
    return (a << 16) | (b & 0xFFFF)


def both_halves(value, lane, first):
    other = pltpu.roll(value, 64, 1)
    return jnp.where((lane < 64) == first, value, other)


def tables(w_ref_value, lane, part, first):
    k = part(w_ref_value)
    sine, cosine = sin_cos(k)
    cosine = both_halves(cosine, lane, first)
    sine = both_halves(sine, lane, first)
    return cosine, jnp.where(lane < 64, -sine, sine)


def level(x0, x1, m0, m1, weights, rot0, rot1):
    g = x0.shape[0]
    shape = (g, 8, 16, 128)
    rows = g * 128

    def split(x, m):
        xf = x.astype(jnp.float32)
        one = xf * jnp.broadcast_to(m[:, :, None, :], shape)
        return (xf - one).astype(jnp.bfloat16).reshape(rows, 128), one.astype(jnp.bfloat16).reshape(rows, 128)

    a0, a1 = split(x0, m0)
    b0, b1 = split(x1, m1)
    lhs = jnp.concatenate([a0, b0, a1, b1], axis=1)
    s = jnp.dot(lhs, weights, preferred_element_type=jnp.float32)
    outs = []
    for half, (c, sn) in enumerate((rot0, rot1)):
        v = s[:, half * 128:(half + 1) * 128]
        r = pltpu.roll(v, 64, 1)
        c = jnp.broadcast_to(c[:, :, None, :], shape).reshape(rows, 128)
        sn = jnp.broadcast_to(sn[:, :, None, :], shape).reshape(rows, 128)
        outs.append((v * c + r * sn).reshape(shape))
    return outs


def kernel(coef, ph, cls, wts_hbm, ev, out,
           wts, aux, a_co, a_aux, b_send, b_co, b_aux, cs3, ms3, cs5, ms5, osend,
           wsem, loc, sa, ra, ra2, sb, rb, sb2, rb2, so, ro, lb):
    s = lax.axis_index("src")
    t = lax.axis_index("tgt")
    y, zl = s % 4, s // 4
    c, zh, x = t % 2, (t // 2) % 2, t // 4
    ys = [(y + d) % 4 for d in range(4)]
    xs = [(x + d) % 4 for d in range(4)]
    zls = [(zl + d) % 4 for d in range(4)]
    cs = [c, 1 - c]
    zhs = [zh, 1 - zh]

    def dev(dx=0, dy=0, dl=0, dh=0, dc=0):
        return zls[dl] * 4 + ys[dy], xs[dx] * 4 + zhs[dh] * 2 + cs[dc]

    yc_peers = [(dy, dc) for dy in (2, 1, 3, 0) for dc in (0, 1) if (dy, dc) != (0, 0)]
    xz_peers = [(dx, dh, dl) for dx in (2, 1, 3, 0) for dh in (1, 0) for dl in (2, 1, 3, 0) if (dx, dh, dl) != (0, 0, 0)]
    out_peers = [(dx, dh, dc) for dx in (2, 1, 3, 0) for dh in (1, 0) for dc in (0, 1) if (dx, dh, dc) != (0, 0, 0)]

    barrier = pltpu.get_barrier_semaphore()
    count = 0
    for dx, dh, dl in xz_peers:
        pl.semaphore_signal(barrier, inc=1, device_id=dev(dx=dx, dh=dh, dl=dl), device_id_type=MESH)
        count += 1
    for dx, dh, dc in out_peers:
        if dc == 1 and (dx, dh) != (0, 0):
            pl.semaphore_signal(barrier, inc=1, device_id=dev(dx=dx, dh=dh, dc=dc), device_id_type=MESH)
            count += 1
    for dy, dc in yc_peers:
        pl.semaphore_signal(barrier, inc=1, device_id=dev(dy=dy, dc=dc), device_id_type=MESH)
        count += 1

    wcopy = pltpu.make_async_copy(wts_hbm, wts, wsem)
    wcopy.start()

    zeros = jnp.zeros((120, 256), jnp.int32)
    kinds = jnp.concatenate([cls[...], zeros], axis=0).T[:, :64]

    def fixed(l):
        return jnp.round(ph[l] * STEP).astype(jnp.int32)

    q = [fixed(l) for l in range(8)]
    aux[:, 0, 0, :] = jnp.concatenate([word(q[0], q[1]), word(q[2], kinds)], axis=1)
    aux[:, 1, 0, :] = jnp.concatenate([word(q[3], q[4]), word(q[5], q[6])], axis=1)
    aux[:, 2, 0, :] = jnp.concatenate([word(q[7], kinds), jnp.zeros((256, 64), jnp.int32)], axis=1)
    aux_n = aux.reshape(4, 4, 4, 2, 2, 3, 1, 128)

    pl.semaphore_wait(barrier, count)

    me_yc = y * 2 + c
    chunks = [(dx, dh) for dx in (0, 2, 1, 3) for dh in (1, 0)]
    for k, (dx, dh) in enumerate(chunks):
        for dy, dc in yc_peers:
            to = dev(dy=dy, dc=dc)
            pltpu.make_async_remote_copy(
                aux_n.at[:, ys[dy], xs[dx], zhs[dh], cs[dc]], a_aux.at[k, me_yc], sa.at[0], ra2.at[k],
                device_id=to, device_id_type=MESH).start()
            pltpu.make_async_remote_copy(
                coef.at[:, ys[dy], xs[dx], zhs[dh], cs[dc]], a_co.at[k, me_yc], sa.at[1], ra.at[k],
                device_id=to, device_id_type=MESH).start()
        pltpu.make_async_copy(aux_n.at[:, y, xs[dx], zhs[dh], c], a_aux.at[k, me_yc], loc.at[k]).start()
        pltpu.make_async_copy(coef.at[:, y, xs[dx], zhs[dh], c], a_co.at[k, me_yc], loc.at[8 + k]).start()
    wcopy.wait()

    lane = lax.broadcasted_iota(jnp.int32, (8, 128), 1)

    def kind_rows(words, at):
        return jnp.broadcast_to(low(words)[:, at:at + 1], (8, 128)).astype(jnp.float32)

    me_slot = (xs[0] // 2, xs[0] % 2, zh, zl // 2, zl % 2)
    for k, (dx, dh) in enumerate(chunks):
        me = (s, t)
        pltpu.make_async_copy(aux_n.at[:, y, xs[dx], zhs[dh], c], a_aux.at[k, me_yc], loc.at[k]).wait()
        pltpu.make_async_copy(coef.at[:, y, xs[dx], zhs[dh], c], a_co.at[k, me_yc], loc.at[8 + k]).wait()
        pltpu.make_async_remote_copy(a_aux.at[k, pl.ds(0, 7)], a_aux.at[k, pl.ds(0, 7)], sa.at[0], ra2.at[k], device_id=me, device_id_type=MESH).wait_recv()
        pltpu.make_async_remote_copy(a_co.at[k, pl.ds(0, 7)], a_co.at[k, pl.ds(0, 7)], sa.at[1], ra.at[k], device_id=me, device_id_type=MESH).wait_recv()
        for dl in (2, 1, 3, 0):
            src = a_aux.at[k, :, zls[dl], pl.ds(1, 2)]
            if (dx, dh, dl) == (0, 0, 0):
                pltpu.make_async_copy(src, b_aux.at[me_slot], lb.at[0]).start()
            else:
                pltpu.make_async_remote_copy(src, b_aux.at[me_slot], sb2, rb2, device_id=dev(dx=dx, dh=dh, dl=dl), device_id_type=MESH).start()
        for n in range(4):
            w = a_aux[k, :, n, 0, 0, :]
            for l, (part, first) in enumerate(((high, True), (low, True), (high, False))):
                co, si = tables(w, lane, part, first)
                cs3[l, 0, n] = co
                cs3[l, 1, n] = si
                ms3[l, n] = kind_rows(w, 64 + l)
        cur = [a_co[k, b] for b in range(8)]
        for l, bit in enumerate((1, 0, 2)):
            step = 1 << bit
            lows = [b for b in range(8) if not b & step]

            def rows(table, chosen):
                return jnp.stack([table[:, b] for b in chosen], axis=1)

            highs = [b + step for b in lows]
            x0 = jnp.stack([cur[b] for b in lows], axis=1)
            x1 = jnp.stack([cur[b] for b in highs], axis=1)
            co, si, mm = cs3[l, 0], cs3[l, 1], ms3[l]
            shape = (4, 4, 16, 128)

            def split(v, m):
                vf = v.astype(jnp.float32)
                one = vf * jnp.broadcast_to(m[:, :, None, :], shape)
                return (vf - one).astype(jnp.bfloat16).reshape(256, 128), one.astype(jnp.bfloat16).reshape(256, 128)

            a0, a1 = split(x0, rows(mm, lows))
            b0, b1 = split(x1, rows(mm, highs))
            lhs = jnp.concatenate([a0, b0, a1, b1], axis=1)
            z = jnp.dot(lhs, wts[l], preferred_element_type=jnp.float32)
            nxt = [None] * 8
            for half, chosen in enumerate((lows, highs)):
                v = z[:, half * 128:(half + 1) * 128]
                r = pltpu.roll(v, 64, 1)
                cc = jnp.broadcast_to(rows(co, chosen)[:, :, None, :], shape).reshape(256, 128)
                ss = jnp.broadcast_to(rows(si, chosen)[:, :, None, :], shape).reshape(256, 128)
                o = (v * cc + r * ss).astype(jnp.bfloat16).reshape(shape)
                for j, b in enumerate(chosen):
                    nxt[b] = o[:, j]
            cur = nxt
        for b in range(8):
            b_send[k, :, b] = cur[b]
        for dl in (2, 1, 3, 0):
            src = b_send.at[k, zls[dl]]
            if (dx, dh, dl) == (0, 0, 0):
                pltpu.make_async_copy(src, b_co.at[me_slot], lb.at[1]).start()
            else:
                pltpu.make_async_remote_copy(src, b_co.at[me_slot], sb, rb, device_id=dev(dx=dx, dh=dh, dl=dl), device_id_type=MESH).start()

    me = (s, t)
    aux_w = a_aux.at[0, :, pl.ds(0, 4), pl.ds(1, 2)]
    pltpu.make_async_copy(a_aux.at[0, :, 0, pl.ds(1, 2)], b_aux.at[me_slot], lb.at[0]).wait()
    b_aux31 = b_aux.reshape(32, 8, 2, 1, 128).at[pl.ds(0, 31)]
    b_co31 = b_co.reshape(32, 8, 16, 128).at[pl.ds(0, 31)]
    arrived = pltpu.make_async_remote_copy(b_aux31, b_aux31, sb2, rb2, device_id=me, device_id_type=MESH)
    arrived.wait_recv()
    arrived.wait_send()
    flat_aux = b_aux.reshape(32, 8, 2, 1, 128)
    flat_cs = cs5.reshape(5, 2, 32, 8, 128)
    flat_ms = ms5.reshape(5, 32, 8, 128)

    @pl.loop(0, 32)
    def _(i):
        w1 = flat_aux[i, :, 0, 0, :]
        w2 = flat_aux[i, :, 1, 0, :]
        for l, (w, part, first) in enumerate(((w1, high, True), (w1, low, True), (w1, high, False), (w1, low, False), (w2, high, True))):
            co, si = tables(w, lane, part, first)
            flat_cs[l, 0, i] = co
            flat_cs[l, 1, i] = si
            flat_ms[l, i] = kind_rows(w2, 3 + l)

    pltpu.make_async_copy(b_send.at[0, 0], b_co.at[me_slot], lb.at[1]).wait()
    got = pltpu.make_async_remote_copy(b_co31, b_co31, sb, rb, device_id=me, device_id_type=MESH)
    got.wait_recv()
    got.wait_send()

    ev_w = ev[...]
    for l, dim in enumerate((2, 4, 1, 3, 0)):
        rest = [d for d in range(5) if d != dim]
        la, lb_ = (rest[0], rest[1])
        w = wts[3 + l]

        @pl.loop(0, 4)
        def _(i):
            def index(bit):
                at = [slice(None)] * 5
                at[la], at[lb_], at[dim] = i // 2, i % 2, bit
                return tuple(at)

            def grab(ref, lead, bit):
                v = ref[lead + index(bit)]
                return v.reshape((4,) + v.shape[2:])

            x0, x1 = grab(b_co, (), 0), grab(b_co, (), 1)
            m0, m1 = grab(ms5, (l,), 0), grab(ms5, (l,), 1)
            r0 = (grab(cs5, (l, 0), 0), grab(cs5, (l, 1), 0))
            r1 = (grab(cs5, (l, 0), 1), grab(cs5, (l, 1), 1))
            o0, o1 = level(x0, x1, m0, m1, w, r0, r1)
            b_co[index(0)] = o0.astype(jnp.bfloat16).reshape(2, 2, 8, 16, 128)
            b_co[index(1)] = o1.astype(jnp.bfloat16).reshape(2, 2, 8, 16, 128)

    for cc in range(2):
        acc = jnp.zeros((128, 128), jnp.float32)
        for zz in range(4):
            for yy in range(4):
                v = b_co[:, :, :, zz // 2, zz % 2, yy * 2 + cc].reshape(128, 128)
                acc = acc + jnp.dot(v, ev_w, preferred_element_type=jnp.float32)
        osend[:, cc] = acc.astype(jnp.bfloat16).reshape(8, 16, 128)
    sends = []
    for dx, dh, dc in out_peers:
        tx = xs[dx] * 2 + zhs[dh]
        cp = pltpu.make_async_remote_copy(osend.at[tx, cs[dc]], out.at[t], so, ro, device_id=dev(dx=dx, dh=dh, dc=dc), device_id_type=MESH)
        cp.start()
    own = pltpu.make_async_copy(osend.at[x * 2 + zh, c], out.at[t], lb.at[2])
    own.start()
    own.wait()
    o15 = out.at[pl.ds(0, 15)]
    fin = pltpu.make_async_remote_copy(o15, o15, so, ro, device_id=me, device_id_type=MESH)
    fin.wait_send()
    fin.wait_recv()
    fa = pltpu.make_async_remote_copy(a_aux.at[pl.ds(0, 7)], a_aux.at[pl.ds(0, 7)], sa.at[0], ra2.at[0], device_id=me, device_id_type=MESH)
    fa.wait_send()
    fb = pltpu.make_async_remote_copy(a_co.at[pl.ds(0, 7)], a_co.at[pl.ds(0, 7)], sa.at[1], ra.at[0], device_id=me, device_id_type=MESH)
    fb.wait_send()


def per_device(coefficients, phases, classes, blocks, evaluation):
    coef = coefficients.reshape(4, 4, 4, 2, 2, 16, 128)
    wts = blocks.reshape(8, 512, 256)
    vmem = pl.BlockSpec(memory_space=pltpu.VMEM)
    anym = pl.BlockSpec(memory_space=pl.ANY)
    bf, f32, i32 = jnp.bfloat16, jnp.float32, jnp.int32
    dma = pltpu.SemaphoreType.DMA
    result = pl.pallas_call(
        kernel,
        out_shape=jax.ShapeDtypeStruct((16, 16, 128), bf),
        in_specs=[anym, vmem, vmem, anym, vmem],
        out_specs=vmem,
        scratch_shapes=[
            pltpu.VMEM((8, 512, 256), bf),
            pltpu.VMEM((256, 3, 1, 128), i32),
            pltpu.VMEM((8, 8, 4, 16, 128), bf),
            pltpu.VMEM((8, 8, 4, 3, 1, 128), i32),
            pltpu.VMEM((8, 4, 8, 16, 128), bf),
            pltpu.VMEM((2, 2, 2, 2, 2, 8, 16, 128), bf),
            pltpu.VMEM((2, 2, 2, 2, 2, 8, 2, 1, 128), i32),
            pltpu.VMEM((3, 2, 4, 8, 128), f32),
            pltpu.VMEM((3, 4, 8, 128), f32),
            pltpu.VMEM((5, 2, 2, 2, 2, 2, 2, 8, 128), f32),
            pltpu.VMEM((5, 2, 2, 2, 2, 2, 8, 128), f32),
            pltpu.VMEM((8, 2, 16, 128), bf),
            dma, dma((16,)), dma((2,)), dma((8,)), dma((8,)),
            dma, dma, dma, dma, dma, dma, dma((3,)),
        ],
        compiler_params=pltpu.CompilerParams(
            collective_id=0, has_side_effects=True, vmem_limit_bytes=48 * 1024 * 1024),
    )(coef, phases, classes, wts, evaluation)
    return result[None]


def solution(mesh):
    placed = (
        P(("src", "tgt"), None, None),
        P(None, ("src", "tgt"), None),
        P(None, ("src", "tgt")),
        P(),
        P(),
    )
    return jax.shard_map(
        per_device, mesh=mesh, in_specs=placed,
        out_specs=P("tgt", "src", None, None), check_vma=False,
    )
```

```python
import jax
import jax.numpy as jnp
from jax import lax
from jax.experimental import pallas as pl
from jax.experimental.pallas import tpu as pltpu
from jax.sharding import PartitionSpec as P

MESH = pl.DeviceIdType.MESH
SIN = (3.1415927410125732, -5.167712688446045, 2.5501604080200195, -0.5992423295974731,
       0.08208189159631729, -0.007275315932929516, 0.0003952804545406252)
COS = (1.0, -4.93480110168457, 4.058694839477539, -1.3351584672927856,
       0.23502980172634125, -0.025358984246850014, 0.0015939107397571206)
STEP = 10430.378350470453


def horner(coefs, v):
    acc = jnp.full_like(v, coefs[-1])
    for a in coefs[-2::-1]:
        acc = acc * v + a
    return acc


def sin_cos(k):
    u = k.astype(jnp.float32) * (1.0 / 32768.0)
    v = u * u
    return u * horner(SIN, v), horner(COS, v)


def high(w):
    return w >> 16


def low(w):
    return (w << 16) >> 16


def word(a, b):
    return (a << 16) | (b & 0xFFFF)


def tables(k, left, second=True):
    sine, cosine = sin_cos(k)
    sine_r, cosine_r = pltpu.roll(sine, 64, 1), pltpu.roll(cosine, 64, 1)
    out = [(jnp.where(left, cosine, cosine_r), jnp.where(left, -sine, sine_r))]
    if second:
        out.append((jnp.where(left, cosine_r, cosine), jnp.where(left, -sine_r, sine)))
    return out


def expand(rows):
    return jnp.broadcast_to(rows[..., None, :], rows.shape[:-1] + (16, 128))


def butterfly(x0, x1, m0, m1, weights, rot0, rot1):
    g, h = x0.shape[:2]
    shape, rows = (g, h, 16, 128), g * h * 16

    def split(x, m):
        one = x * expand(m).astype(jnp.bfloat16)
        return (x - one).reshape(rows, 128), one.reshape(rows, 128)

    a0, a1 = split(x0, m0)
    b0, b1 = split(x1, m1)
    s = jnp.dot(jnp.concatenate([a0, b0, a1, b1], axis=1), weights, preferred_element_type=jnp.float32)
    outs = []
    for half, (c, sn) in enumerate((rot0, rot1)):
        v = s[:, half * 128:(half + 1) * 128]
        outs.append((v.reshape(shape) * expand(c) + pltpu.roll(v, 64, 1).reshape(shape) * expand(sn)))
    return outs


def kernel(coef, ph_hbm, cls_hbm, wts_hbm, ev_hbm, out,
           ph, cls, ev, wts, aux, a_co, a_aux, b_send, b_co, b_aux, cs3, ms3, cs5, ms5, osend,
           wsem, loc, sa, ra, ra2, sb, rb, sb2, rb2, so, ro, lb, known):
    copies = [pltpu.make_async_copy(a, b, wsem.at[i]) for i, (a, b) in enumerate(
        ((ph_hbm, ph), (cls_hbm, cls), (wts_hbm, wts), (ev_hbm, ev)))]
    for cp in copies:
        cp.start()
    s = lax.axis_index("src")
    t = lax.axis_index("tgt")
    y, zl = s % 4, s // 4
    c, zh, x = t % 2, (t // 2) % 2, t // 4
    x1, x0 = x // 2, x % 2
    ys = [(y + d) % 4 for d in range(4)]
    xs = [x, x1 * 2 + 1 - x0, (1 - x1) * 2 + x0, 3 - x]
    zls = [(zl + d) % 4 for d in range(4)]
    cs = [c, 1 - c]
    zhs = [zh, 1 - zh]
    me = (s, t)

    def dev(dx=0, dy=0, dl=0, dh=0, dc=0):
        return zls[dl] * 4 + ys[dy], xs[dx] * 4 + zhs[dh] * 2 + cs[dc]

    yc_peers = [(dy, dc) for dy in (2, 1, 3, 0) for dc in (0, 1) if (dy, dc) != (0, 0)]
    z_peers = [(dh, dl) for dh in (1, 0) for dl in (0, 2, 1, 3) if (dh, dl) != (0, 0)]
    x_peers = (2, 1, 3)

    barrier = pltpu.get_barrier_semaphore()
    for dh, dl in z_peers:
        pl.semaphore_signal(barrier, inc=1, device_id=dev(dh=dh, dl=dl), device_id_type=MESH)
    for dx in x_peers:
        pl.semaphore_signal(barrier, inc=1, device_id=dev(dx=dx), device_id_type=MESH)
    for dy, dc in yc_peers:
        pl.semaphore_signal(barrier, inc=1, device_id=dev(dy=dy, dc=dc), device_id_type=MESH)

    copies[0].wait()
    copies[1].wait()
    kinds = jnp.concatenate([cls[...], jnp.zeros((56, 256), jnp.int32)], axis=0)

    def fixed(l):
        return jnp.round(ph[l] * STEP).astype(jnp.int32)

    q = [fixed(l) for l in range(8)]
    aux[:, 0, 0, :] = jnp.concatenate([word(q[0], q[1]), word(q[2], kinds)], axis=0).T
    aux[:, 1, 0, :] = jnp.concatenate([word(q[3], q[4]), word(q[5], q[6])], axis=0).T
    aux[:, 2, 0, :] = jnp.concatenate([word(q[7], kinds), jnp.zeros((64, 256), jnp.int32)], axis=0).T
    aux_n = aux.reshape(4, 4, 4, 2, 2, 3, 1, 128)

    pl.semaphore_wait(barrier, 17)
    for dx in x_peers:
        pl.semaphore_signal(known, inc=1, device_id=dev(dx=dx), device_id_type=MESH)

    me_yc = y * 2 + c
    chunks = [(dx, dh) for dx in (2, 3, 1, 0) for dh in (1, 0)]
    for dy, dc in yc_peers:
        pltpu.make_async_remote_copy(
            aux_n.at[:, ys[dy], :, :, cs[dc]], a_aux.at[me_yc], sa.at[0], ra2,
            device_id=dev(dy=dy, dc=dc), device_id_type=MESH).start()
    own_aux = pltpu.make_async_copy(aux_n.at[:, y, :, :, c], a_aux.at[me_yc], lb.at[0])
    own_aux.start()
    own_co = []
    for k, (dx, dh) in enumerate(chunks):
        for dy, dc in yc_peers:
            pltpu.make_async_remote_copy(
                coef.at[:, ys[dy], xs[dx], zhs[dh], cs[dc]], a_co.at[k, me_yc], sa.at[1], ra.at[k],
                device_id=dev(dy=dy, dc=dc), device_id_type=MESH).start()
        own_co.append(pltpu.make_async_copy(coef.at[:, y, xs[dx], zhs[dh], c], a_co.at[k, me_yc], loc.at[k]))
        own_co[-1].start()
    copies[2].wait()
    copies[3].wait()

    def recv(ref, sem, send=False):
        cp = pltpu.make_async_remote_copy(ref, ref, sem, sem, device_id=me, device_id_type=MESH)
        if send:
            cp.wait_send()
        else:
            cp.wait_recv()

    me_slot = (x1, x0, zh, zl // 2, zl % 2)

    def pass_on(k, chunk, src_of, dst, ssem, rsem):
        dx, dh = chunk
        for dl in (2, 1, 3, 0):
            if (dx, dh, dl) == (0, 0, 0):
                pltpu.make_async_copy(src_of(zls[dl]), dst.at[me_slot], rsem.at[k]).start()
            else:
                pltpu.make_async_remote_copy(
                    src_of(zls[dl]), dst.at[me_slot], ssem, rsem.at[k],
                    device_id=dev(dx=dx, dh=dh, dl=dl), device_id_type=MESH).start()

    own_aux.wait()
    recv(a_aux.at[pl.ds(0, 7)], ra2)
    pl.semaphore_wait(known, 3)
    for k, (dx, dh) in enumerate(chunks):
        pass_on(k, (dx, dh), lambda z: a_aux.at[:, z, xs[dx], zhs[dh], pl.ds(1, 2)], b_aux, sb2, rb2)

    left = lax.broadcasted_iota(jnp.int32, (8, 128), 1) < 64

    def kind_rows(words, at):
        return jnp.broadcast_to(low(words)[:, at:at + 1], (8, 128)).astype(jnp.float32)

    for k, (dx, dh) in enumerate(chunks):
        for n in range(4):
            w = a_aux[:, n, xs[dx], zhs[dh], 0, 0, :]
            first, third = tables(high(w), left)
            second, = tables(low(w), left, False)
            for l, (co, si) in enumerate((first, second, third)):
                cs3[l, 0, n] = co
                cs3[l, 1, n] = si
                ms3[l, n] = kind_rows(w, 64 + l)
        own_co[k].wait()
        recv(a_co.at[k, pl.ds(0, 7)], ra.at[k])
        cur = [a_co[k, b] for b in range(8)]
        for l, bit in enumerate((1, 0, 2)):
            lows = [b for b in range(8) if not b & (1 << bit)]
            highs = [b + (1 << bit) for b in lows]

            def rows(table, chosen):
                return jnp.stack([table[:, b] for b in chosen], axis=0)

            def boxes(chosen):
                return jnp.stack([cur[b] for b in chosen], axis=0)

            co, si, mm = cs3[l, 0], cs3[l, 1], ms3[l]
            o0, o1 = butterfly(boxes(lows), boxes(highs), rows(mm, lows), rows(mm, highs), wts[l],
                               (rows(co, lows), rows(si, lows)), (rows(co, highs), rows(si, highs)))
            o0, o1 = o0.astype(jnp.bfloat16), o1.astype(jnp.bfloat16)
            for j in range(4):
                cur[lows[j]], cur[highs[j]] = o0[j], o1[j]
        for b in range(8):
            b_send[k, :, b] = cur[b]
        pass_on(k, (dx, dh), lambda z: b_send.at[k, z], b_co, sb, rb)

    def step(l, dim, fixed_at):
        def grab(ref, lead, bit):
            at = [slice(None)] * 5
            at[dim] = bit
            for d, v in fixed_at.items():
                at[d] = v
            v = ref[tuple(lead) + tuple(at)]
            return v.reshape((4,) + v.shape[2:])

        rots = [tuple(grab(cs5, (l - 3, i), bit) for i in range(2)) for bit in range(2)]
        return butterfly(grab(b_co, (), 0), grab(b_co, (), 1), grab(ms5, (l - 3,), 0), grab(ms5, (l - 3,), 1), wts[l], *rots)

    def step_in_place(l, dim, fixed_at):
        for bit, o in enumerate(step(l, dim, fixed_at)):
            at = [slice(None)] * 5
            at[dim] = bit
            for d, v in fixed_at.items():
                at[d] = v
            b_co[tuple(at)] = o.astype(jnp.bfloat16).reshape(2, 2, 8, 16, 128)

    @pl.loop(0, 4)
    def _(i):
        gx1 = (x1 + 1 + i // 2) % 2
        gx0 = (x0 + i // 2 + i % 2) % 2
        for h in range(2):
            recv(b_aux.at[gx1, gx0, zhs[1 - h]], rb2.at[i * 2 + h])

        @pl.loop(0, 8)
        def _(j):
            at = (gx1, gx0, j // 4, (j // 2) % 2, j % 2)
            w1 = b_aux[at + (slice(None), 0, 0)]
            w2 = b_aux[at + (slice(None), 1, 0)]
            l3, l5 = tables(high(w1), left)
            l4, l6 = tables(low(w1), left)
            l7, = tables(high(w2), left, False)
            for l, (co, si) in enumerate((l3, l4, l5, l6, l7)):
                cs5[(l, 0) + at] = co
                cs5[(l, 1) + at] = si
                ms5[(l,) + at] = kind_rows(w2, 3 + l)

        for h in range(2):
            recv(b_co.at[gx1, gx0, zhs[1 - h]], rb.at[i * 2 + h])
        step_in_place(3, 2, {0: gx1, 1: gx0})
        step_in_place(4, 4, {0: gx1, 1: gx0})

        @pl.when(i % 2 == 1)
        def _():
            for b in range(2):
                step_in_place(5, 1, {0: gx1, 2: b})
            for b in range(2):
                step_in_place(6, 3, {0: gx1, 1: b})

    ev_w = ev[...]
    for dh in (1, 0):
        for dx0 in (1, 0):
            qx0 = (x0 + dx0) % 2
            sums = []
            for o in step(7, 0, {1: qx0, 2: zhs[dh]}):
                sums.append(o.reshape(16, 2, 16, 128).sum(axis=0).reshape(32, 128))
            total = jnp.concatenate(sums, axis=0)
            big = total.astype(jnp.bfloat16)
            small = (total - big.astype(jnp.float32)).astype(jnp.bfloat16)
            r = (jnp.dot(big, ev_w, preferred_element_type=jnp.float32)
                 + jnp.dot(small, ev_w, preferred_element_type=jnp.float32)).astype(jnp.bfloat16)
            osend[:, qx0, zhs[dh]] = r.reshape(2, 2, 16, 128)
            for dx1 in (1, 0):
                for dc in (0, 1):
                    src = osend.at[(x1 + dx1) % 2, qx0, zhs[dh], cs[dc]]
                    if (dx1, dx0, dh, dc) == (0, 0, 0, 0):
                        pltpu.make_async_copy(src, out.at[t], ro).start()
                    else:
                        pltpu.make_async_remote_copy(
                            src, out.at[t], so, ro, device_id=dev(dx=dx1 * 2 + dx0, dh=dh, dc=dc), device_id_type=MESH).start()
    recv(b_aux.reshape(32, 8, 2, 1, 128).at[pl.ds(0, 31)], sb2, True)
    recv(b_co.reshape(32, 8, 16, 128).at[pl.ds(0, 31)], sb, True)
    recv(a_aux.at[pl.ds(0, 7)], sa.at[0], True)
    recv(a_co.at[pl.ds(0, 7)], sa.at[1], True)
    recv(out.at[pl.ds(0, 15)], so, True)
    recv(out, ro)


def per_device(coefficients, phases, classes, blocks, evaluation):
    coef = coefficients.reshape(4, 4, 4, 2, 2, 16, 128)
    wts = blocks.reshape(8, 512, 256)
    vmem = pl.BlockSpec(memory_space=pltpu.VMEM)
    hbm = pl.BlockSpec(memory_space=pltpu.HBM)
    bf, f32, i32 = jnp.bfloat16, jnp.float32, jnp.int32
    dma = pltpu.SemaphoreType.DMA
    result = pl.pallas_call(
        kernel,
        out_shape=jax.ShapeDtypeStruct((16, 16, 128), bf),
        in_specs=[hbm] * 5,
        out_specs=vmem,
        scratch_shapes=[
            pltpu.VMEM((8, 64, 256), f32),
            pltpu.VMEM((8, 256), i32),
            pltpu.VMEM((128, 128), bf),
            pltpu.VMEM((8, 512, 256), bf),
            pltpu.VMEM((256, 3, 1, 128), i32),
            pltpu.VMEM((8, 8, 4, 16, 128), bf),
            pltpu.VMEM((8, 4, 4, 2, 3, 1, 128), i32),
            pltpu.VMEM((8, 4, 8, 16, 128), bf),
            pltpu.VMEM((2, 2, 2, 2, 2, 8, 16, 128), bf),
            pltpu.VMEM((2, 2, 2, 2, 2, 8, 2, 1, 128), i32),
            pltpu.VMEM((3, 2, 4, 8, 128), f32),
            pltpu.VMEM((3, 4, 8, 128), f32),
            pltpu.VMEM((5, 2, 2, 2, 2, 2, 2, 8, 128), f32),
            pltpu.VMEM((5, 2, 2, 2, 2, 2, 8, 128), f32),
            pltpu.VMEM((2, 2, 2, 2, 16, 128), bf),
            dma((4,)), dma((8,)), dma((2,)), dma((8,)), dma,
            dma, dma((8,)), dma, dma((8,)), dma, dma, dma((1,)),
            pltpu.SemaphoreType.REGULAR,
        ],
        compiler_params=pltpu.CompilerParams(
            collective_id=0, has_side_effects=True, vmem_limit_bytes=67043328),
    )(coef, phases.transpose(0, 2, 1), classes, wts, evaluation)
    return result[None]


def solution(mesh):
    placed = (
        P(("src", "tgt"), None, None),
        P(None, ("src", "tgt"), None),
        P(None, ("src", "tgt")),
        P(),
        P(),
    )
    return jax.shard_map(
        per_device, mesh=mesh, in_specs=placed,
        out_specs=P("tgt", "src", None, None), check_vma=False,
    )
```

```python
import jax
import jax.numpy as jnp
from jax import lax
from jax.experimental import pallas as pl
from jax.experimental.pallas import tpu as pltpu
from jax.sharding import PartitionSpec as P

MESH = pl.DeviceIdType.MESH
SIN = (3.1415927410125732, -5.167712688446045, 2.5501604080200195, -0.5992423295974731,
       0.08208189159631729, -0.007275315932929516, 0.0003952804545406252)
COS = (1.0, -4.93480110168457, 4.058694839477539, -1.3351584672927856,
       0.23502980172634125, -0.025358984246850014, 0.0015939107397571206)
STEP = 10430.378350470453


def horner(coefs, v):
    acc = jnp.full_like(v, coefs[-1])
    for a in coefs[-2::-1]:
        acc = acc * v + a
    return acc


def sin_cos(k):
    u = k.astype(jnp.float32) * (1.0 / 32768.0)
    v = u * u
    return u * horner(SIN, v), horner(COS, v)


def high(w):
    return w >> 16


def low(w):
    return (w << 16) >> 16


def word(a, b):
    return (a << 16) | (b & 0xFFFF)


def tables(k, left, second=True):
    sine, cosine = sin_cos(k)
    sine_r, cosine_r = pltpu.roll(sine, 64, 1), pltpu.roll(cosine, 64, 1)
    out = [(jnp.where(left, cosine, cosine_r), jnp.where(left, -sine, sine_r))]
    if second:
        out.append((jnp.where(left, cosine_r, cosine), jnp.where(left, -sine_r, sine)))
    return out


def expand(rows):
    return jnp.broadcast_to(rows[..., None, :], rows.shape[:-1] + (16, 128))


def butterfly(x0, x1, m0, m1, weights, rot0, rot1):
    g, h = x0.shape[:2]
    shape, rows = (g, h, 16, 128), g * h * 16

    def split(x, m):
        one = x * expand(m).astype(jnp.bfloat16)
        return (x - one).reshape(rows, 128), one.reshape(rows, 128)

    a0, a1 = split(x0, m0)
    b0, b1 = split(x1, m1)
    s = jnp.dot(jnp.concatenate([a0, b0, a1, b1], axis=1), weights, preferred_element_type=jnp.float32)
    outs = []
    for half, (c, sn) in enumerate((rot0, rot1)):
        v = s[:, half * 128:(half + 1) * 128]
        outs.append((v.reshape(shape) * expand(c) + pltpu.roll(v, 64, 1).reshape(shape) * expand(sn)))
    return outs


def kernel(coef, ph_hbm, cls_hbm, wts_hbm, ev_hbm, out,
           ph, cls, ev, wts, aux, a_co, a_aux, p_send, b_send, b_co, b_aux, q_co, q_aux, qa, cs3, ms3, cs5, ms5, osend,
           wsem, loc, sa, ra, ra2, sb, rb, sb2, rb2, so, ro, lb, known, sq, rq, rq2, sqa, rqa):
    copies = [pltpu.make_async_copy(a, b, wsem.at[i]) for i, (a, b) in enumerate(
        ((ph_hbm, ph), (cls_hbm, cls), (wts_hbm, wts), (ev_hbm, ev)))]
    for cp in copies:
        cp.start()
    s = lax.axis_index("src")
    t = lax.axis_index("tgt")
    y, zl = s % 4, s // 4
    c, zh, x = t % 2, (t // 2) % 2, t // 4
    x1, x0 = x // 2, x % 2
    ys = [(y + d) % 4 for d in range(4)]
    xs = [x, x1 * 2 + 1 - x0, (1 - x1) * 2 + x0, 3 - x]
    z = zh * 4 + zl
    zs = [(z + d) % 8 for d in range(8)]
    ns = [(z + d + 6) % 8 for d in range(8)]
    n1s, nhs = [v % 4 // 2 for v in ns], [v // 4 for v in ns]
    zl0s = [zl % 2, 1 - zl % 2]
    cs = [c, 1 - c]
    zhs = [zh, 1 - zh]
    me = (s, t)

    def dev(dx=0, dy=0, dz=0, dc=0):
        return zs[dz] % 4 * 4 + ys[dy], xs[dx] * 4 + zs[dz] // 4 * 2 + cs[dc]

    yc_peers = [(dy, dc) for dy in (2, 1, 3, 0) for dc in (0, 1) if (dy, dc) != (0, 0)]
    z_peers = (4, 3, 5, 2, 6, 1, 7)
    x_peers = (2, 1, 3)

    barrier = pltpu.get_barrier_semaphore()
    for dz in z_peers:
        pl.semaphore_signal(barrier, inc=1, device_id=dev(dz=dz), device_id_type=MESH)
    for dx in x_peers:
        pl.semaphore_signal(barrier, inc=1, device_id=dev(dx=dx), device_id_type=MESH)
    for dy, dc in yc_peers:
        pl.semaphore_signal(barrier, inc=1, device_id=dev(dy=dy, dc=dc), device_id_type=MESH)

    copies[0].wait()
    copies[1].wait()
    kinds = jnp.concatenate([cls[...], jnp.zeros((56, 256), jnp.int32)], axis=0)

    def fixed(l):
        return jnp.round(ph[l] * STEP).astype(jnp.int32)

    q = [fixed(l) for l in range(8)]
    aux[:, 0, 0, :] = jnp.concatenate([word(q[0], q[1]), word(q[2], kinds)], axis=0).T
    aux[:, 1, 0, :] = jnp.concatenate([word(q[3], q[4]), word(q[5], q[6])], axis=0).T
    aux[:, 2, 0, :] = jnp.concatenate([word(q[7], kinds), jnp.zeros((64, 256), jnp.int32)], axis=0).T
    aux_n = aux.reshape(2, 2, 4, 4, 2, 2, 3, 1, 128)

    pl.semaphore_wait(barrier, 17)
    for dx in x_peers:
        pl.semaphore_signal(known, inc=1, device_id=dev(dx=dx), device_id_type=MESH)

    for dz in (3, 5, 1, 7):
        at = (n1s[dz], zl0s[1], slice(None), x, nhs[dz], slice(None))
        pltpu.make_async_remote_copy(
            aux_n.at[at], q_aux.at[zl // 2, zh], sq.at[0], rq2, device_id=dev(dz=dz), device_id_type=MESH).start()
        pltpu.make_async_remote_copy(
            coef.at[at], q_co.at[zl // 2, zh], sq.at[1], rq, device_id=dev(dz=dz), device_id_type=MESH).start()

    me_yc = y * 2 + c
    groups = (2, 3, 1, 0)
    own_aux, own_co = [], {}

    def part(g):
        return slice(None) if g < 3 else zl0s[0]

    def parities(g):
        return (1, 0) if g < 3 else (0,)

    for g, dx in enumerate(groups):
        for dy, dc in yc_peers:
            pltpu.make_async_remote_copy(
                aux_n.at[:, part(g), ys[dy], xs[dx], :, cs[dc]], a_aux.at[g, me_yc, :, part(g)], sa.at[0], ra2.at[g],
                device_id=dev(dy=dy, dc=dc), device_id_type=MESH).start()
        own_aux.append(pltpu.make_async_copy(aux_n.at[:, part(g), y, xs[dx], :, c], a_aux.at[g, me_yc, :, part(g)], lb.at[g]))
        own_aux[-1].start()
        for p in parities(g):
            k = g * 2 + 1 - p
            for dy, dc in yc_peers:
                pltpu.make_async_remote_copy(
                    coef.at[:, zl0s[p], ys[dy], xs[dx], :, cs[dc]], a_co.at[k, me_yc], sa.at[1], ra.at[k],
                    device_id=dev(dy=dy, dc=dc), device_id_type=MESH).start()
            own_co[k] = pltpu.make_async_copy(coef.at[:, zl0s[p], y, xs[dx], :, c], a_co.at[k, me_yc], loc.at[k])
            own_co[k].start()
    copies[2].wait()
    copies[3].wait()

    def recv(ref, sem, send=False):
        cp = pltpu.make_async_remote_copy(ref, ref, sem, sem, device_id=me, device_id_type=MESH)
        if send:
            cp.wait_send()
        else:
            cp.wait_recv()

    me_slot = (x1, x0, zh, zl // 2, zl % 2)

    def pass_on(dx, dz, src, dst, ssem, rsem):
        if (dx, dz) == (0, 0):
            pltpu.make_async_copy(src, dst.at[me_slot], rsem).start()
        else:
            pltpu.make_async_remote_copy(
                src, dst.at[me_slot], ssem, rsem, device_id=dev(dx=dx, dz=dz), device_id_type=MESH).start()

    pl.semaphore_wait(known, 3)
    left = lax.broadcasted_iota(jnp.int32, (8, 128), 1) < 64

    def kind_rows(words, at):
        return jnp.broadcast_to(low(words)[:, at:at + 1], (8, 128)).astype(jnp.float32)

    def pack(w, v, ref, at):
        ref[at + (0,)] = w[:4]
        ref[at + (1,)] = w[4:]
        ref[at + (2,)] = jnp.where(left[:4], v[:4], pltpu.roll(v, 64, 1)[4:])

    def early_levels(words, chunk):
        for n, w in enumerate(words):
            first, third = tables(high(w), left)
            second, = tables(low(w), left, False)
            for l, (co, si) in enumerate((first, second, third)):
                cs3[l, 0, n] = co
                cs3[l, 1, n] = si
                ms3[l, n] = kind_rows(w, 64 + l)
        cur = chunk()
        for l, bit in enumerate((1, 0, 2)):
            lows = [b for b in range(8) if not b & (1 << bit)]
            highs = [b + (1 << bit) for b in lows]

            def rows(table, chosen):
                return jnp.stack([table[:, b] for b in chosen], axis=0)

            def boxes(chosen):
                return jnp.stack([cur[b] for b in chosen], axis=0)

            co, si, mm = cs3[l, 0], cs3[l, 1], ms3[l]
            o0, o1 = butterfly(boxes(lows), boxes(highs), rows(mm, lows), rows(mm, highs), wts[l],
                               (rows(co, lows), rows(si, lows)), (rows(co, highs), rows(si, highs)))
            o0, o1 = o0.astype(jnp.bfloat16), o1.astype(jnp.bfloat16)
            for j in range(4):
                cur[lows[j]], cur[highs[j]] = o0[j], o1[j]
        return cur

    def chunk_of(k, own):
        def load():
            own.wait()
            recv(a_co.at[k, pl.ds(0, 7)], ra.at[k])
            return [a_co[k, b].reshape(4, 16, 128) for b in range(8)]
        return load

    for g, dx in enumerate(groups):
        own_aux[g].wait()
        recv(a_aux.at[g, pl.ds(0, 7), :, part(g)], ra2.at[g])
        for i in range(8) if g < 3 else range(4):
            n1, n0, nh = (i // 4, i // 2 % 2, i % 2) if g < 3 else (i // 2, zl0s[0], i % 2)
            pack(a_aux[g, :, n1, n0, nh, 1, 0, :], a_aux[g, :, n1, n0, nh, 2, 0, :], p_send, (g, n1, n0, nh))
        for dz in (4, 3, 5, 2, 6, 1, 7, 0) if g < 3 else (4, 2, 6, 0):
            pass_on(dx, dz, p_send.at[g, n1s[dz], zl0s[dz % 2], nhs[dz]], b_aux, sb2, rb2.at[g])
        for p in parities(g):
            k = g * 2 + 1 - p
            cur = early_levels([a_aux[g, :, n // 2, zl0s[p], n % 2, 0, 0, :] for n in range(4)], chunk_of(k, own_co[k]))
            for b in range(8):
                b_send[k, :, b] = cur[b]
            for dz in (3, 5, 1, 7) if p else (4, 2, 6, 0):
                pass_on(dx, dz, b_send.at[k, n1s[dz] * 2 + nhs[dz]], b_co, sb, rb.at[k])
        if g == 0:
            recv(q_aux, rq2)
            recv(q_co, rq)
            for dy, dc in yc_peers:
                to = dev(dy=dy, dc=dc)
                pltpu.make_async_remote_copy(
                    q_aux.at[:, :, ys[dy], cs[dc]], qa.at[me_yc], sqa, rqa, device_id=to, device_id_type=MESH).start()
                pltpu.make_async_remote_copy(
                    q_co.at[:, :, ys[dy], cs[dc]], a_co.at[6, me_yc], sa.at[1], ra.at[6], device_id=to, device_id_type=MESH).start()
            own_qa = pltpu.make_async_copy(q_aux.at[:, :, y, c], qa.at[me_yc], loc.at[8])
            own_qa.start()
            own_q = pltpu.make_async_copy(q_co.at[:, :, y, c], a_co.at[6, me_yc], loc.at[6])
            own_q.start()

    own_qa.wait()
    recv(qa.at[pl.ds(0, 7)], rqa)
    for i in range(4):
        pack(qa[:, i // 2, i % 2, 1, 0, :], qa[:, i // 2, i % 2, 2, 0, :], b_aux, (x1, x0, i % 2, i // 2, zl0s[1]))
    cur = early_levels([qa[:, n // 2, n % 2, 0, 0, :] for n in range(4)], chunk_of(6, own_q))
    for n in range(4):
        for b in range(8):
            b_co[x1, x0, n % 2, n // 2, zl0s[1], b] = cur[b][n]

    def step(l, dim, fixed_at):
        def grab(ref, lead, bit):
            at = [slice(None)] * 5
            at[dim] = bit
            for d, v in fixed_at.items():
                at[d] = v
            v = ref[tuple(lead) + tuple(at)]
            return v.reshape((-1,) + v.shape[-3 + (ref is not b_co):])

        rots = [tuple(grab(cs5, (l - 3, i), bit) for i in range(2)) for bit in range(2)]
        return butterfly(grab(b_co, (), 0), grab(b_co, (), 1), grab(ms5, (l - 3,), 0), grab(ms5, (l - 3,), 1), wts[l], *rots)

    def step_in_place(l, dim, fixed_at):
        for bit, o in enumerate(step(l, dim, fixed_at)):
            at = [slice(None)] * 5
            at[dim] = bit
            for d, v in fixed_at.items():
                at[d] = v
            b_co[tuple(at)] = o.astype(jnp.bfloat16).reshape((2,) * (4 - len(fixed_at)) + (8, 16, 128))

    @pl.loop(0, 4)
    def _(i):
        gx1 = (x1 + 1 + i // 2) % 2
        gx0 = (x0 + i // 2 + i % 2) % 2
        @pl.when(i < 3)
        def _():
            recv(b_aux.at[gx1, gx0], rb2.at[i])

        @pl.when(i == 3)
        def _():
            recv(b_aux.at[x1, x0, :, :, zl0s[0]], rb2.at[3])

        @pl.loop(0, 8)
        def _(j):
            at = (gx1, gx0, j // 4, (j // 2) % 2, j % 2)
            w1 = jnp.concatenate([b_aux[at + (0,)], b_aux[at + (1,)]], axis=0)
            w2 = b_aux[at + (2,)]
            w2 = jnp.concatenate([w2, pltpu.roll(w2, 64, 1)], axis=0)
            l3, l5 = tables(high(w1), left)
            l4, l6 = tables(low(w1), left)
            l7, = tables(high(w2), left, False)
            for l, (co, si) in enumerate((l3, l4, l5, l6, l7)):
                cs5[(l, 0) + at] = co
                cs5[(l, 1) + at] = si
                ms5[(l,) + at] = kind_rows(w2, 3 + l)

        for h in range(2):
            if h:
                recv(b_co.at[gx1, gx0, :, :, zl0s[0]], rb.at[i * 2 + 1])
            else:
                @pl.when(i < 3)
                def _():
                    recv(b_co.at[gx1, gx0, :, :, zl0s[1]], rb.at[i * 2])
            step_in_place(3, 2, {0: gx1, 1: gx0, 4: zl0s[1 - h]})
        step_in_place(4, 4, {0: gx1, 1: gx0})

        @pl.when(i % 2 == 1)
        def _():
            for b in range(2):
                step_in_place(5, 1, {0: gx1, 2: b})
            for b in range(2):
                step_in_place(6, 3, {0: gx1, 1: b})

    ev_w = ev[...]
    mine = x * 4 + nhs[0] * 2 + c
    for dx0 in (0, 1):
        for dh in (1, 0):
            qx0 = (x0 + dx0) % 2
            sums = []
            for o in step(7, 0, {1: qx0, 2: zhs[dh]}):
                sums.append(o.reshape(16, 2, 16, 128).sum(axis=0).reshape(32, 128))
            total = jnp.concatenate(sums, axis=0)
            big = total.astype(jnp.bfloat16)
            small = (total - big.astype(jnp.float32)).astype(jnp.bfloat16)
            r = (jnp.dot(big, ev_w, preferred_element_type=jnp.float32)
                 + jnp.dot(small, ev_w, preferred_element_type=jnp.float32)).astype(jnp.bfloat16)
            osend[:, qx0, zhs[dh]] = r.reshape(2, 2, 16, 128)
            for dx1 in (1, 0):
                for dc in (0, 1):
                    src = osend.at[(x1 + dx1) % 2, qx0, zhs[dh], cs[dc]]
                    to = (ns[0] % 4 * 4 + y, xs[dx1 * 2 + dx0] * 4 + zhs[dh] * 2 + cs[dc])
                    pltpu.make_async_remote_copy(src, out.at[mine], so, ro, device_id=to, device_id_type=MESH).start()
    recv(b_aux.reshape(32, 3, 4, 128).at[pl.ds(0, 27)], sb2, True)
    recv(b_co.reshape(32, 8, 16, 128).at[pl.ds(0, 27)], sb, True)
    recv(aux.at[pl.ds(0, 196)], sa.at[0], True)
    recv(a_co.at[pl.ds(0, 7)], sa.at[1], True)
    recv(q_aux, sq.at[0], True)
    recv(q_co, sq.at[1], True)
    recv(qa.at[pl.ds(0, 7)], sqa, True)
    recv(out, so, True)
    recv(out, ro)


def per_device(coefficients, phases, classes, blocks, evaluation):
    coef = coefficients.reshape(2, 2, 4, 4, 2, 2, 16, 128)
    wts = blocks.reshape(8, 512, 256)
    vmem = pl.BlockSpec(memory_space=pltpu.VMEM)
    hbm = pl.BlockSpec(memory_space=pltpu.HBM)
    bf, f32, i32 = jnp.bfloat16, jnp.float32, jnp.int32
    dma = pltpu.SemaphoreType.DMA
    result = pl.pallas_call(
        kernel,
        out_shape=pltpu.VMEM((16, 16, 128), bf),
        in_specs=[hbm] * 5,
        out_specs=vmem,
        scratch_shapes=[
            pltpu.VMEM((8, 64, 256), f32),
            pltpu.VMEM((8, 256), i32),
            pltpu.VMEM((128, 128), bf),
            pltpu.VMEM((8, 512, 256), bf),
            pltpu.VMEM((256, 3, 1, 128), i32),
            pltpu.VMEM((8, 8, 2, 2, 16, 128), bf),
            pltpu.VMEM((4, 8, 2, 2, 2, 3, 1, 128), i32),
            pltpu.VMEM((4, 2, 2, 2, 3, 4, 128), i32),
            pltpu.VMEM((8, 4, 8, 16, 128), bf),
            pltpu.VMEM((2, 2, 2, 2, 2, 8, 16, 128), bf),
            pltpu.VMEM((2, 2, 2, 2, 2, 3, 4, 128), i32),
            pltpu.VMEM((2, 2, 4, 2, 16, 128), bf),
            pltpu.VMEM((2, 2, 4, 2, 3, 1, 128), i32),
            pltpu.VMEM((8, 2, 2, 3, 1, 128), i32),
            pltpu.VMEM((3, 2, 4, 8, 128), f32),
            pltpu.VMEM((3, 4, 8, 128), f32),
            pltpu.VMEM((5, 2, 2, 2, 2, 2, 2, 8, 128), f32),
            pltpu.VMEM((5, 2, 2, 2, 2, 2, 8, 128), f32),
            pltpu.VMEM((2, 2, 2, 2, 16, 128), bf),
            dma((4,)), dma((9,)), dma((2,)), dma((8,)), dma((4,)),
            dma, dma((8,)), dma, dma((4,)), dma, dma, dma((4,)),
            pltpu.SemaphoreType.REGULAR, dma((2,)), dma, dma, dma, dma,
        ],
        compiler_params=pltpu.CompilerParams(
            collective_id=0, has_side_effects=True, vmem_limit_bytes=66912256),
    )(coef, phases.transpose(0, 2, 1), classes, wts, evaluation)
    return result[None]


def solution(mesh):
    placed = (
        P(("src", "tgt"), None, None),
        P(None, ("src", "tgt"), None),
        P(None, ("src", "tgt")),
        P(),
        P(),
    )
    return jax.shard_map(
        per_device, mesh=mesh, in_specs=placed,
        out_specs=P("tgt", "src", None, None), check_vma=False,
    )
```

```python
import jax
import jax.numpy as jnp
from jax import lax
from jax.experimental import pallas as pl
from jax.experimental.pallas import tpu as pltpu
from jax.sharding import PartitionSpec as P

MESH = pl.DeviceIdType.MESH
SIN = (3.141592502593994, -5.167698860168457, 2.5499982833862305, -0.59855055809021, 0.0807478204369545, -0.00608947454020381)
COS = (1.0, -4.93480110168457, 4.058694839477539, -1.3351584672927856, 0.23502980172634125, -0.025358984246850014, 0.0015939107397571206)
STEP = 10430.378350470453


def horner(coefs, v):
    acc = jnp.full_like(v, coefs[-1])
    for a in coefs[-2::-1]:
        acc = acc * v + a
    return acc


def sin_cos(k):
    u = k.astype(jnp.float32) * (1.0 / 32768.0)
    v = u * u
    return u * horner(SIN, v), horner(COS, v)


def high(w):
    return w >> 16


def low(w):
    return (w << 16) >> 16


def word(a, b):
    return (a << 16) | (b & 0xFFFF)


def tables(k, left, second=True):
    sine, cosine = sin_cos(k)
    sine_r, cosine_r = pltpu.roll(sine, 64, 1), pltpu.roll(cosine, 64, 1)
    out = [(jnp.where(left, cosine, cosine_r), jnp.where(left, -sine, sine_r))]
    if second:
        out.append((jnp.where(left, cosine_r, cosine), jnp.where(left, -sine_r, sine)))
    return out


def expand(rows):
    return jnp.broadcast_to(rows[..., None, :], rows.shape[:-1] + (16, 128))


def butterfly(x0, x1, m0, m1, weights, rot0, rot1):
    g, h = x0.shape[:2]
    shape, rows = (g, h, 16, 128), g * h * 16

    def split(x, m):
        one = x * expand(m).astype(jnp.bfloat16)
        return (x - one).reshape(rows, 128), one.reshape(rows, 128)

    a0, a1 = split(x0, m0)
    b0, b1 = split(x1, m1)
    s = jnp.dot(jnp.concatenate([a0, b0, a1, b1], axis=1), weights, preferred_element_type=jnp.float32)
    outs = []
    for half, (c, sn) in enumerate((rot0, rot1)):
        v = s[:, half * 128:(half + 1) * 128]
        outs.append((v.reshape(shape) * expand(c) + pltpu.roll(v, 64, 1).reshape(shape) * expand(sn)))
    return outs


def kernel(coef, ph_hbm, cls_hbm, wts_hbm, ev_hbm, out,
           ph, cls, ev, wts, aux, a_co, a_aux, p_send, b_send, b_co, b_aux, q_co, q_aux, qa, cs3, ms3, cs5, ms5, acc, osend,
           wsem, loc, sa, ra, ra2, sb, rb, sb2, rb2, so, ro, lb, known, sq, rq, rq2, sqa, rqa):
    copies = [pltpu.make_async_copy(a, b, wsem.at[i]) for i, (a, b) in enumerate(
        ((ph_hbm, ph), (cls_hbm, cls), (wts_hbm, wts), (ev_hbm, ev)))]
    for cp in copies:
        cp.start()
    s = lax.axis_index("src")
    t = lax.axis_index("tgt")
    y, zl = s % 4, s // 4
    c, zh, x = t % 2, (t // 2) % 2, t // 4
    x1, x0 = x // 2, x % 2
    ys = [(y + d) % 4 for d in range(4)]
    xs = [x, x1 * 2 + 1 - x0, (1 - x1) * 2 + x0, 3 - x]
    z = zh * 4 + zl
    zs = [(z + d) % 8 for d in range(8)]
    ns = [(z + d + 6) % 8 for d in range(8)]
    n1s, nhs = [v % 4 // 2 for v in ns], [v // 4 for v in ns]
    zl0s = [zl % 2, 1 - zl % 2]
    cs = [c, 1 - c]
    zhs = [zh, 1 - zh]
    me = (s, t)

    def dev(dx=0, dy=0, dz=0, dc=0):
        return zs[dz] % 4 * 4 + ys[dy], xs[dx] * 4 + zs[dz] // 4 * 2 + cs[dc]

    yc_peers = [(dy, dc) for dy in (2, 1, 3, 0) for dc in (0, 1) if (dy, dc) != (0, 0)]
    z_peers = (4, 3, 5, 2, 6, 1, 7)
    x_peers = (2, 1, 3)

    barrier = pltpu.get_barrier_semaphore()
    for dz in z_peers:
        pl.semaphore_signal(barrier, inc=1, device_id=dev(dz=dz), device_id_type=MESH)
    for dx in x_peers:
        pl.semaphore_signal(barrier, inc=1, device_id=dev(dx=dx), device_id_type=MESH)
    for dy, dc in yc_peers:
        pl.semaphore_signal(barrier, inc=1, device_id=dev(dy=dy, dc=dc), device_id_type=MESH)

    copies[0].wait()
    copies[1].wait()
    kinds = jnp.concatenate([cls[...], jnp.zeros((56, 256), jnp.int32)], axis=0)

    def fixed(l):
        return jnp.round(ph[l] * STEP).astype(jnp.int32)

    q = [fixed(l) for l in range(8)]
    aux[:, 0, 0, :] = jnp.concatenate([word(q[0], q[1]), word(q[2], kinds)], axis=0).T
    aux[:, 1, 0, :] = jnp.concatenate([word(q[3], q[4]), word(q[5], q[6])], axis=0).T
    aux[:, 2, 0, :] = jnp.concatenate([word(q[7], kinds), jnp.zeros((64, 256), jnp.int32)], axis=0).T
    aux_n = aux.reshape(2, 2, 4, 4, 2, 2, 3, 1, 128)

    pl.semaphore_wait(barrier, 17)
    for dx in x_peers:
        pl.semaphore_signal(known, inc=1, device_id=dev(dx=dx), device_id_type=MESH)

    for dz in (3, 5, 1, 7):
        at = (n1s[dz], zl0s[1], slice(None), x, nhs[dz], slice(None))
        pltpu.make_async_remote_copy(
            aux_n.at[at], q_aux.at[zl // 2, zh], sq.at[0], rq2, device_id=dev(dz=dz), device_id_type=MESH).start()
        pltpu.make_async_remote_copy(
            coef.at[at], q_co.at[zl // 2, zh], sq.at[1], rq, device_id=dev(dz=dz), device_id_type=MESH).start()

    me_yc = y * 2 + c
    groups = (2, 3, 1, 0)
    own_aux, own_co = [], {}

    def part(g):
        return slice(None) if g < 3 else zl0s[0]

    def parities(g):
        return (1, 0) if g < 3 else (0,)

    for g, dx in enumerate(groups):
        for dy, dc in yc_peers:
            pltpu.make_async_remote_copy(
                aux_n.at[:, part(g), ys[dy], xs[dx], :, cs[dc]], a_aux.at[g, :, part(g), :, :, pl.ds(me_yc, 1)], sa.at[0], ra2.at[g],
                device_id=dev(dy=dy, dc=dc), device_id_type=MESH).start()
        own_aux.append(pltpu.make_async_copy(aux_n.at[:, part(g), y, xs[dx], :, c], a_aux.at[g, :, part(g), :, :, pl.ds(me_yc, 1)], lb.at[g]))
        own_aux[-1].start()
        for p in parities(g):
            k = g * 2 + 1 - p
            for dy, dc in yc_peers:
                pltpu.make_async_remote_copy(
                    coef.at[:, zl0s[p], ys[dy], xs[dx], :, cs[dc]], a_co.at[k, me_yc], sa.at[1], ra.at[k],
                    device_id=dev(dy=dy, dc=dc), device_id_type=MESH).start()
            own_co[k] = pltpu.make_async_copy(coef.at[:, zl0s[p], y, xs[dx], :, c], a_co.at[k, me_yc], loc.at[k])
            own_co[k].start()
    copies[2].wait()
    copies[3].wait()

    def recv(ref, sem, send=False):
        cp = pltpu.make_async_remote_copy(ref, ref, sem, sem, device_id=me, device_id_type=MESH)
        if send:
            cp.wait_send()
        else:
            cp.wait_recv()

    me_slot = (x1, x0, zh, zl // 2, zl % 2)

    def pass_on(dx, dz, src, dst, ssem, rsem, half=()):
        if (dx, dz) == (0, 0):
            pltpu.make_async_copy(src, dst.at[me_slot + half], rsem).start()
        else:
            pltpu.make_async_remote_copy(
                src, dst.at[me_slot + half], ssem, rsem, device_id=dev(dx=dx, dz=dz), device_id_type=MESH).start()

    pl.semaphore_wait(known, 3)
    left = lax.broadcasted_iota(jnp.int32, (8, 128), 1) < 64

    def kind_rows(words, at):
        return jnp.broadcast_to(low(words)[:, at:at + 1], (8, 128)).astype(jnp.float32)

    def pack(w, v, ref, at):
        ref[at + (0,)] = w[:4]
        ref[at + (1,)] = w[4:]
        ref[at + (2,)] = jnp.where(left[:4], v[:4], pltpu.roll(v, 64, 1)[4:])

    def pass_chunk(k, dx, p, hf):
        for dz in (3, 5, 1, 7) if p else (4, 2, 6, 0):
            pass_on(dx, dz, b_send.at[k, n1s[dz] * 2 + nhs[dz], pl.ds(hf * 4, 4)], b_co, sb, rb.at[k, hf], (hf,))

    def early_levels(words, chunk):
        for n, w in enumerate(words):
            first, third = tables(high(w), left)
            second, = tables(low(w), left, False)
            for l, (co, si) in enumerate((first, second, third)):
                cs3[l, 0, n] = co
                cs3[l, 1, n] = si
                ms3[l, n] = kind_rows(w, 64 + l)
        cur = chunk()
        for l, bit in enumerate((1, 0, 2)):
            lows = [b for b in range(8) if not b & (1 << bit)]
            highs = [b + (1 << bit) for b in lows]

            def rows(table, chosen):
                return jnp.stack([table[:, b] for b in chosen], axis=0)

            def boxes(chosen):
                return jnp.stack([cur[b] for b in chosen], axis=0)

            co, si, mm = cs3[l, 0], cs3[l, 1], ms3[l]
            o0, o1 = butterfly(boxes(lows), boxes(highs), rows(mm, lows), rows(mm, highs), wts[l],
                               (rows(co, lows), rows(si, lows)), (rows(co, highs), rows(si, highs)))
            o0, o1 = o0.astype(jnp.bfloat16), o1.astype(jnp.bfloat16)
            for j in range(4):
                cur[lows[j]], cur[highs[j]] = o0[j], o1[j]
        return cur

    def chunk_of(k, own):
        def load():
            own.wait()
            recv(a_co.at[k, pl.ds(0, 7)], ra.at[k])
            return [a_co[k, b].reshape(4, 16, 128) for b in range(8)]
        return load

    for g, dx in enumerate(groups):
        own_aux[g].wait()
        recv(aux.at[pl.ds(0, 56 if g < 3 else 28)], ra2.at[g])
        for i in range(8) if g < 3 else range(4):
            n1, n0, nh = (i // 4, i // 2 % 2, i % 2) if g < 3 else (i // 2, zl0s[0], i % 2)
            pack(a_aux[g, n1, n0, nh, 1], a_aux[g, n1, n0, nh, 2], p_send, (g, n1, n0, nh))
        for dz in (4, 3, 5, 2, 6, 1, 7, 0) if g < 3 else (4, 2, 6, 0):
            pass_on(dx, dz, p_send.at[g, n1s[dz], zl0s[dz % 2], nhs[dz]], b_aux, sb2, rb2.at[g])
        for p in parities(g):
            k = g * 2 + 1 - p
            cur = early_levels([a_aux[g, n // 2, zl0s[p], n % 2, 0] for n in range(4)], chunk_of(k, own_co[k]))
            for b in range(8):
                b_send[k, :, b] = cur[b]
            pass_chunk(k, dx, p, 0)
            if g < 2:
                pass_chunk(k, dx, p, 1)
        if g == 0:
            recv(q_aux, rq2)
            recv(q_co, rq)
            for dy, dc in yc_peers:
                to = dev(dy=dy, dc=dc)
                pltpu.make_async_remote_copy(
                    q_aux.at[:, :, ys[dy], cs[dc]], qa.at[:, :, :, pl.ds(me_yc, 1)], sqa, rqa, device_id=to, device_id_type=MESH).start()
                pltpu.make_async_remote_copy(
                    q_co.at[:, :, ys[dy], cs[dc]], a_co.at[6, me_yc], sa.at[1], ra.at[6], device_id=to, device_id_type=MESH).start()
            own_qa = pltpu.make_async_copy(q_aux.at[:, :, y, c], qa.at[:, :, :, pl.ds(me_yc, 1)], loc.at[8])
            own_qa.start()
            own_q = pltpu.make_async_copy(q_co.at[:, :, y, c], a_co.at[6, me_yc], loc.at[6])
            own_q.start()

    pass_chunk(4, 1, 1, 1)
    pass_chunk(5, 1, 0, 1)
    pass_chunk(7, 0, 0, 1)
    own_qa.wait()
    recv(aux.at[pl.ds(0, 28)], rqa)
    for i in range(4):
        pack(qa[i // 2, i % 2, 1], qa[i // 2, i % 2, 2], b_aux, (x1, x0, i % 2, i // 2, zl0s[1]))
    cur = early_levels([qa[n // 2, n % 2, 0] for n in range(4)], chunk_of(6, own_q))
    for n in range(4):
        for b in range(8):
            b_co[x1, x0, n % 2, n // 2, zl0s[1], b // 4, b % 4] = cur[b][n]

    def place(dim, bit, fixed_at):
        at = [slice(None)] * 5
        at[dim] = bit
        for d, v in fixed_at.items():
            at[d] = v
        return tuple(at)

    def step(l, dim, fixed_at, hf):
        height = 8 if hf is None else 4

        def boxes(bit):
            at = place(dim, bit, fixed_at)
            return b_co[at if hf is None else at + (hf,)].reshape(-1, height, 16, 128)

        def rows(ref, lead, bit):
            at = lead + place(dim, bit, fixed_at)
            return ref[at if hf is None else at + (pl.ds(hf * 4, 4),)].reshape(-1, height, 128)

        rots = [tuple(rows(cs5, (l - 3, i), bit) for i in range(2)) for bit in range(2)]
        return butterfly(boxes(0), boxes(1), rows(ms5, (l - 3,), 0), rows(ms5, (l - 3,), 1), wts[l], *rots)

    def step_in_place(l, dim, fixed_at, hf=None):
        for bit, o in enumerate(step(l, dim, fixed_at, hf)):
            at = place(dim, bit, fixed_at)
            lead = (2,) * (4 - len(fixed_at))
            if hf is None:
                b_co[at] = o.astype(jnp.bfloat16).reshape(lead + (2, 4, 16, 128))
            else:
                b_co[at + (hf,)] = o.astype(jnp.bfloat16).reshape(lead + (4, 16, 128))

    def late_tables(gx1, gx0):
        @pl.loop(0, 2)
        def _(z1):
          for j in range(4):
            at = (gx1, gx0, j // 2, z1, j % 2)
            w1 = jnp.concatenate([b_aux[at + (0,)], b_aux[at + (1,)]], axis=0)
            w2 = b_aux[at + (2,)]
            w2 = jnp.concatenate([w2, pltpu.roll(w2, 64, 1)], axis=0)
            l3, l5 = tables(high(w1), left)
            l4, l6 = tables(low(w1), left)
            l7, = tables(high(w2), left, False)
            for l, (co, si) in enumerate((l3, l4, l5, l6, l7)):
                cs5[(l, 0) + at] = co
                cs5[(l, 1) + at] = si
                ms5[(l,) + at] = kind_rows(w2, 3 + l)

    far = 1 - x1

    @pl.loop(0, 2)
    def _(i):
        gx0 = (x0 + i) % 2
        recv(b_aux.at[far, gx0], rb2.at[i])
        late_tables(far, gx0)
        for h in range(2):
            for hf in range(2):
                recv(b_co.at[far, gx0, :, :, zl0s[1 - h], hf], rb.at[i * 2 + h, hf])
            step_in_place(3, 2, {0: far, 1: gx0, 4: zl0s[1 - h]})
        step_in_place(4, 4, {0: far, 1: gx0})

    for b in range(2):
        step_in_place(5, 1, {0: far, 2: b})
    for b in range(2):
        step_in_place(6, 3, {0: far, 1: b})

    near = 1 - x0
    recv(b_aux.at[x1, near], rb2.at[2])
    late_tables(x1, near)
    recv(b_aux.at[x1, x0, :, :, zl0s[0]], rb2.at[3])
    late_tables(x1, x0)
    step_in_place(3, 2, {0: x1, 1: x0, 4: zl0s[1]})
    ev_w = ev[...]
    mine = x * 4 + nhs[0] * 2 + c
    for hf in range(2):
        for h in range(2):
            recv(b_co.at[x1, near, :, :, zl0s[1 - h], hf], rb.at[4 + h, hf])
            step_in_place(3, 2, {0: x1, 1: near, 4: zl0s[1 - h]}, hf)
        step_in_place(4, 4, {0: x1, 1: near}, hf)
        recv(b_co.at[x1, x0, :, :, zl0s[0], hf], rb.at[7, hf])
        step_in_place(3, 2, {0: x1, 1: x0, 4: zl0s[0]}, hf)
        step_in_place(4, 4, {0: x1, 1: x0}, hf)
        step_in_place(5, 1, {0: x1}, hf)
        step_in_place(6, 3, {0: x1}, hf)
        sums = [[o.reshape(2, 4, 2, 2, 16, 128).sum(axis=(1, 2)) for o in step(7, 0, {1: q}, hf)] for q in range(2)]
        if hf == 0:
            for q in range(2):
                for bit in range(2):
                    acc[bit, q] = sums[q][bit]
            continue
        total = jnp.concatenate([(sums[q][bit] + acc[bit, q]).reshape(64, 128) for bit in range(2) for q in range(2)], axis=0)
        big = total.astype(jnp.bfloat16)
        small = (total - big.astype(jnp.float32)).astype(jnp.bfloat16)
        r = (jnp.dot(big, ev_w, preferred_element_type=jnp.float32)
             + jnp.dot(small, ev_w, preferred_element_type=jnp.float32)).astype(jnp.bfloat16)
        osend[...] = r.reshape(2, 2, 2, 2, 16, 128)
        for dx in (2, 3, 1, 0):
            for dh in (1, 0):
                for dc in (0, 1):
                    to = (ns[0] % 4 * 4 + y, xs[dx] * 4 + zhs[dh] * 2 + cs[dc])
                    pltpu.make_async_remote_copy(
                        osend.at[xs[dx] // 2, xs[dx] % 2, zhs[dh], cs[dc]], out.at[mine], so, ro,
                        device_id=to, device_id_type=MESH).start()
    recv(b_aux.reshape(32, 3, 4, 128).at[pl.ds(0, 27)], sb2, True)
    recv(b_co.reshape(32, 8, 16, 128).at[pl.ds(0, 27)], sb, True)
    recv(aux.at[pl.ds(0, 196)], sa.at[0], True)
    recv(a_co.at[pl.ds(0, 7)], sa.at[1], True)
    recv(q_aux, sq.at[0], True)
    recv(q_co, sq.at[1], True)
    recv(aux.at[pl.ds(0, 28)], sqa, True)
    recv(out, so, True)
    recv(out, ro)


def per_device(coefficients, phases, classes, blocks, evaluation):
    coef = coefficients.reshape(2, 2, 4, 4, 2, 2, 16, 128)
    wts = blocks.reshape(8, 512, 256)
    vmem = pl.BlockSpec(memory_space=pltpu.VMEM)
    hbm = pl.BlockSpec(memory_space=pltpu.HBM)
    bf, f32, i32 = jnp.bfloat16, jnp.float32, jnp.int32
    dma = pltpu.SemaphoreType.DMA
    result = pl.pallas_call(
        kernel,
        out_shape=pltpu.VMEM((16, 16, 128), bf),
        in_specs=[hbm] * 5,
        out_specs=vmem,
        scratch_shapes=[
            pltpu.VMEM((8, 64, 256), f32),
            pltpu.VMEM((8, 256), i32),
            pltpu.VMEM((128, 128), bf),
            pltpu.VMEM((8, 512, 256), bf),
            pltpu.VMEM((256, 3, 1, 128), i32),
            pltpu.VMEM((8, 8, 2, 2, 16, 128), bf),
            pltpu.VMEM((4, 2, 2, 2, 3, 8, 128), i32),
            pltpu.VMEM((4, 2, 2, 2, 3, 4, 128), i32),
            pltpu.VMEM((8, 4, 8, 16, 128), bf),
            pltpu.VMEM((2, 2, 2, 2, 2, 2, 4, 16, 128), bf),
            pltpu.VMEM((2, 2, 2, 2, 2, 3, 4, 128), i32),
            pltpu.VMEM((2, 2, 4, 2, 16, 128), bf),
            pltpu.VMEM((2, 2, 4, 2, 3, 1, 128), i32),
            pltpu.VMEM((2, 2, 3, 8, 128), i32),
            pltpu.VMEM((3, 2, 4, 8, 128), f32),
            pltpu.VMEM((3, 4, 8, 128), f32),
            pltpu.VMEM((5, 2, 2, 2, 2, 2, 2, 8, 128), f32),
            pltpu.VMEM((5, 2, 2, 2, 2, 2, 8, 128), f32),
            pltpu.VMEM((2, 2, 2, 2, 16, 128), f32),
            pltpu.VMEM((2, 2, 2, 2, 16, 128), bf),
            dma((4,)), dma((9,)), dma((2,)), dma((8,)), dma((4,)),
            dma, dma((8, 2)), dma, dma((4,)), dma, dma, dma((4,)),
            pltpu.SemaphoreType.REGULAR, dma((2,)), dma, dma, dma, dma,
        ],
        compiler_params=pltpu.CompilerParams(
            collective_id=0, has_side_effects=True, vmem_limit_bytes=66912256),
    )(coef, phases.transpose(0, 2, 1), classes, wts, evaluation)
    return result[None]


def solution(mesh):
    placed = (
        P(("src", "tgt"), None, None),
        P(None, ("src", "tgt"), None),
        P(None, ("src", "tgt")),
        P(),
        P(),
    )
    return jax.shard_map(
        per_device, mesh=mesh, in_specs=placed,
        out_specs=P("tgt", "src", None, None), check_vma=False,
    )
```

```python
import jax
import jax.numpy as jnp
from jax import lax
from jax.experimental import pallas as pl
from jax.experimental.pallas import tpu as pltpu
from jax.sharding import PartitionSpec as P

MESH = pl.DeviceIdType.MESH
SIN = (3.141592502593994, -5.167698860168457, 2.5499982833862305, -0.59855055809021, 0.0807478204369545, -0.00608947454020381)
COS = (1.0, -4.93480110168457, 4.058694839477539, -1.3351584672927856, 0.23502980172634125, -0.025358984246850014, 0.0015939107397571206)
STEP = 10430.378350470453


def horner(coefs, v):
    acc = jnp.full_like(v, coefs[-1])
    for a in coefs[-2::-1]:
        acc = acc * v + a
    return acc


def sin_cos(k):
    u = k.astype(jnp.float32) * (1.0 / 32768.0)
    v = u * u
    return u * horner(SIN, v), horner(COS, v)


def high(w):
    return w >> 16


def low(w):
    return (w << 16) >> 16


def word(a, b):
    return (a << 16) | (b & 0xFFFF)


def tables(k, left, second=True):
    sine, cosine = sin_cos(k)
    sine_r, cosine_r = pltpu.roll(sine, 64, 1), pltpu.roll(cosine, 64, 1)
    out = [(jnp.where(left, cosine, cosine_r), jnp.where(left, -sine, sine_r))]
    if second:
        out.append((jnp.where(left, cosine_r, cosine), jnp.where(left, -sine_r, sine)))
    return out


def expand(rows):
    return jnp.broadcast_to(rows[..., None, :], rows.shape[:-1] + (16, 128))


def butterfly(x0, x1, m0, m1, weights, rot0, rot1):
    g, h = x0.shape[:2]
    shape, rows = (g, h, 16, 128), g * h * 16

    def split(x, m):
        one = x * expand(m).astype(jnp.bfloat16)
        return (x - one).reshape(rows, 128), one.reshape(rows, 128)

    a0, a1 = split(x0, m0)
    b0, b1 = split(x1, m1)
    s = jnp.dot(jnp.concatenate([a0, b0, a1, b1], axis=1), weights, preferred_element_type=jnp.float32)
    outs = []
    for half, (c, sn) in enumerate((rot0, rot1)):
        v = s[:, half * 128:(half + 1) * 128]
        outs.append((v.reshape(shape) * expand(c) + pltpu.roll(v, 64, 1).reshape(shape) * expand(sn)))
    return outs


def kernel(coef, ph_hbm, cls_hbm, wts_hbm, ev_hbm, out,
           ph, cls, ev, wts, aux, a_co, a_aux, p_send, b_send, b_co, b_aux, q_co, q_aux, qa, cs3, ms3, cs5, ms5, acc, osend,
           wsem, loc, sa, ra, ra2, sb, rb, sb2, rb2, so, ro, lb, known, sq, rq, rq2, sqa, rqa):
    copies = [pltpu.make_async_copy(a, b, wsem.at[i]) for i, (a, b) in enumerate(
        ((ph_hbm, ph), (cls_hbm, cls), (wts_hbm, wts), (ev_hbm, ev)))]
    for cp in copies:
        cp.start()
    s = lax.axis_index("src")
    t = lax.axis_index("tgt")
    y, zl = s % 4, s // 4
    c, zh, x = t % 2, (t // 2) % 2, t // 4
    x1, x0 = x // 2, x % 2
    ys = [(y + d) % 4 for d in range(4)]
    xs = [x, x1 * 2 + 1 - x0, (1 - x1) * 2 + x0, 3 - x]
    z = zh * 4 + zl
    zs = [(z + d) % 8 for d in range(8)]
    ns = [(z + d + 6) % 8 for d in range(8)]
    n1s, nhs = [v % 4 // 2 for v in ns], [v // 4 for v in ns]
    zl0s = [zl % 2, 1 - zl % 2]
    cs = [c, 1 - c]
    zhs = [zh, 1 - zh]
    me = (s, t)

    def dev(dx=0, dy=0, dz=0, dc=0):
        return zs[dz] % 4 * 4 + ys[dy], xs[dx] * 4 + zs[dz] // 4 * 2 + cs[dc]

    yc_peers = [(dy, dc) for dy in (2, 1, 3, 0) for dc in (0, 1) if (dy, dc) != (0, 0)]
    z_peers = (4, 3, 5, 2, 6, 1, 7)
    x_peers = (2, 1, 3)

    barrier = pltpu.get_barrier_semaphore()
    for dz in z_peers:
        pl.semaphore_signal(barrier, inc=1, device_id=dev(dz=dz), device_id_type=MESH)
    for dx in x_peers:
        pl.semaphore_signal(barrier, inc=1, device_id=dev(dx=dx), device_id_type=MESH)
    for dy, dc in yc_peers:
        pl.semaphore_signal(barrier, inc=1, device_id=dev(dy=dy, dc=dc), device_id_type=MESH)

    copies[0].wait()
    copies[1].wait()
    kinds = jnp.concatenate([cls[...], jnp.zeros((56, 256), jnp.int32)], axis=0)

    def fixed(l):
        return jnp.round(ph[l] * STEP).astype(jnp.int32)

    q = [fixed(l) for l in range(8)]
    aux[:, 0, 0, :] = jnp.concatenate([word(q[0], q[1]), word(q[2], kinds)], axis=0).T
    aux[:, 1, 0, :] = jnp.concatenate([word(q[3], q[4]), word(q[5], q[6])], axis=0).T
    aux[:, 2, 0, :] = jnp.concatenate([word(q[7], kinds), jnp.zeros((64, 256), jnp.int32)], axis=0).T
    aux_n = aux.reshape(2, 2, 4, 4, 2, 2, 3, 1, 128)

    pl.semaphore_wait(barrier, 17)
    for dx in x_peers:
        pl.semaphore_signal(known, inc=1, device_id=dev(dx=dx), device_id_type=MESH)

    for p in (1, 0):
        for dz in (3, 5, 1, 7) if p else (4, 2, 6, 0):
            at = (n1s[dz], zl0s[p], slice(None), x, nhs[dz], slice(None))
            for src, dst, ssem, rsem in ((aux_n, q_aux, sq.at[0], rq2.at[p]), (coef, q_co, sq.at[1], rq.at[p])):
                if dz == 0:
                    pltpu.make_async_copy(src.at[at], dst.at[p, zl // 2, zh], rsem).start()
                else:
                    pltpu.make_async_remote_copy(
                        src.at[at], dst.at[p, zl // 2, zh], ssem, rsem, device_id=dev(dz=dz), device_id_type=MESH).start()

    me_yc = y * 2 + c
    groups = (2, 3, 1)
    own_aux, own_co = [], {}

    for g, dx in enumerate(groups):
        for dy, dc in yc_peers:
            pltpu.make_async_remote_copy(
                aux_n.at[:, :, ys[dy], xs[dx], :, cs[dc]], a_aux.at[g, :, :, :, :, pl.ds(me_yc, 1)], sa.at[0], ra2.at[g],
                device_id=dev(dy=dy, dc=dc), device_id_type=MESH).start()
        own_aux.append(pltpu.make_async_copy(aux_n.at[:, :, y, xs[dx], :, c], a_aux.at[g, :, :, :, :, pl.ds(me_yc, 1)], lb.at[g]))
        own_aux[-1].start()
        for p in (1, 0):
            k = g * 2 + 1 - p
            for dy, dc in yc_peers:
                pltpu.make_async_remote_copy(
                    coef.at[:, zl0s[p], ys[dy], xs[dx], :, cs[dc]], a_co.at[k, me_yc], sa.at[1], ra.at[k],
                    device_id=dev(dy=dy, dc=dc), device_id_type=MESH).start()
            own_co[k] = pltpu.make_async_copy(coef.at[:, zl0s[p], y, xs[dx], :, c], a_co.at[k, me_yc], loc.at[k])
            own_co[k].start()
    copies[2].wait()
    copies[3].wait()

    def recv(ref, sem, send=False):
        cp = pltpu.make_async_remote_copy(ref, ref, sem, sem, device_id=me, device_id_type=MESH)
        if send:
            cp.wait_send()
        else:
            cp.wait_recv()

    me_slot = (x1, x0, zh, zl // 2, zl % 2)

    def pass_on(dx, dz, src, dst, ssem, rsem, half=()):
        if (dx, dz) == (0, 0):
            pltpu.make_async_copy(src, dst.at[me_slot + half], rsem).start()
        else:
            pltpu.make_async_remote_copy(
                src, dst.at[me_slot + half], ssem, rsem, device_id=dev(dx=dx, dz=dz), device_id_type=MESH).start()

    pl.semaphore_wait(known, 3)
    left = lax.broadcasted_iota(jnp.int32, (8, 128), 1) < 64

    def kind_rows(words, at):
        return jnp.broadcast_to(low(words)[:, at:at + 1], (8, 128)).astype(jnp.float32)

    def pack(w, v, ref, at):
        ref[at + (0,)] = w[:4]
        ref[at + (1,)] = w[4:]
        ref[at + (2,)] = jnp.where(left[:4], v[:4], pltpu.roll(v, 64, 1)[4:])

    def pass_chunk(k, dx, p, hf):
        for dz in (3, 5, 1, 7) if p else (4, 2, 6, 0):
            pass_on(dx, dz, b_send.at[k, n1s[dz] * 2 + nhs[dz], pl.ds(hf * 4, 4)], b_co, sb, rb.at[k, hf], (hf,))

    def early_levels(words, chunk):
        for n, w in enumerate(words):
            first, third = tables(high(w), left)
            second, = tables(low(w), left, False)
            for l, (co, si) in enumerate((first, second, third)):
                cs3[l, 0, n] = co
                cs3[l, 1, n] = si
                ms3[l, n] = kind_rows(w, 64 + l)
        cur = chunk()
        for l, bit in enumerate((1, 0, 2)):
            lows = [b for b in range(8) if not b & (1 << bit)]
            highs = [b + (1 << bit) for b in lows]

            def rows(table, chosen):
                return jnp.stack([table[:, b] for b in chosen], axis=0)

            def boxes(chosen):
                return jnp.stack([cur[b] for b in chosen], axis=0)

            co, si, mm = cs3[l, 0], cs3[l, 1], ms3[l]
            o0, o1 = butterfly(boxes(lows), boxes(highs), rows(mm, lows), rows(mm, highs), wts[l],
                               (rows(co, lows), rows(si, lows)), (rows(co, highs), rows(si, highs)))
            o0, o1 = o0.astype(jnp.bfloat16), o1.astype(jnp.bfloat16)
            for j in range(4):
                cur[lows[j]], cur[highs[j]] = o0[j], o1[j]
        return cur

    def chunk_of(k, own):
        def load():
            own.wait()
            recv(a_co.at[k, pl.ds(0, 7)], ra.at[k])
            return [a_co[k, b].reshape(4, 16, 128) for b in range(8)]
        return load

    own_qa, own_q = {}, {}
    for g, dx in enumerate(groups):
        own_aux[g].wait()
        recv(aux.at[pl.ds(0, 56)], ra2.at[g])
        for i in range(8):
            n1, n0, nh = i // 4, i // 2 % 2, i % 2
            pack(a_aux[g, n1, n0, nh, 1], a_aux[g, n1, n0, nh, 2], p_send, (g, n1, n0, nh))
        for dz in (4, 3, 5, 2, 6, 1, 7, 0):
            pass_on(dx, dz, p_send.at[g, n1s[dz], zl0s[dz % 2], nhs[dz]], b_aux, sb2, rb2.at[g])
        for p in (1, 0):
            k = g * 2 + 1 - p
            cur = early_levels([a_aux[g, n // 2, zl0s[p], n % 2, 0] for n in range(4)], chunk_of(k, own_co[k]))
            for b in range(8):
                b_send[k, :, b] = cur[b]
            pass_chunk(k, dx, p, 0)
            if g < 2:
                pass_chunk(k, dx, p, 1)
        if g < 2:
            q = 1 - g
            recv(q_aux.at[q], rq2.at[q])
            recv(q_co.at[q], rq.at[q])
            for dy, dc in yc_peers:
                to = dev(dy=dy, dc=dc)
                pltpu.make_async_remote_copy(
                    q_aux.at[q, :, :, ys[dy], cs[dc]], qa.at[q, :, :, :, pl.ds(me_yc, 1)], sqa, rqa.at[q],
                    device_id=to, device_id_type=MESH).start()
                pltpu.make_async_remote_copy(
                    q_co.at[q, :, :, ys[dy], cs[dc]], a_co.at[7 - q, me_yc], sa.at[1], ra.at[7 - q],
                    device_id=to, device_id_type=MESH).start()
            own_qa[q] = pltpu.make_async_copy(q_aux.at[q, :, :, y, c], qa.at[q, :, :, :, pl.ds(me_yc, 1)], loc.at[8 + q])
            own_qa[q].start()
            own_q[q] = pltpu.make_async_copy(q_co.at[q, :, :, y, c], a_co.at[7 - q, me_yc], loc.at[7 - q])
            own_q[q].start()

    pass_chunk(4, 1, 1, 1)
    pass_chunk(5, 1, 0, 1)
    for q in (1, 0):
        own_qa[q].wait()
        recv(aux.at[pl.ds(0, 28)], rqa.at[q])
        for i in range(4):
            pack(qa[q, i // 2, i % 2, 1], qa[q, i // 2, i % 2, 2], b_aux, (x1, x0, i % 2, i // 2, zl0s[q]))
        cur = early_levels([qa[q, n // 2, n % 2, 0] for n in range(4)], chunk_of(7 - q, own_q[q]))
        for n in range(4):
            for b in range(8):
                b_co[x1, x0, n % 2, n // 2, zl0s[q], b // 4, b % 4] = cur[b][n]

    def place(dim, bit, fixed_at):
        at = [slice(None)] * 5
        at[dim] = bit
        for d, v in fixed_at.items():
            at[d] = v
        return tuple(at)

    def step(l, dim, fixed_at, hf):
        height = 8 if hf is None else 4

        def boxes(bit):
            at = place(dim, bit, fixed_at)
            return b_co[at if hf is None else at + (hf,)].reshape(-1, height, 16, 128)

        def rows(ref, lead, bit):
            at = lead + place(dim, bit, fixed_at)
            return ref[at if hf is None else at + (pl.ds(hf * 4, 4),)].reshape(-1, height, 128)

        rots = [tuple(rows(cs5, (l - 3, i), bit) for i in range(2)) for bit in range(2)]
        return butterfly(boxes(0), boxes(1), rows(ms5, (l - 3,), 0), rows(ms5, (l - 3,), 1), wts[l], *rots)

    def step_in_place(l, dim, fixed_at, hf=None):
        for bit, o in enumerate(step(l, dim, fixed_at, hf)):
            at = place(dim, bit, fixed_at)
            lead = (2,) * (4 - len(fixed_at))
            if hf is None:
                b_co[at] = o.astype(jnp.bfloat16).reshape(lead + (2, 4, 16, 128))
            else:
                b_co[at + (hf,)] = o.astype(jnp.bfloat16).reshape(lead + (4, 16, 128))

    def late_tables(gx1, gx0):
        @pl.loop(0, 2)
        def _(z1):
          for j in range(4):
            at = (gx1, gx0, j // 2, z1, j % 2)
            w1 = jnp.concatenate([b_aux[at + (0,)], b_aux[at + (1,)]], axis=0)
            w2 = b_aux[at + (2,)]
            w2 = jnp.concatenate([w2, pltpu.roll(w2, 64, 1)], axis=0)
            l3, l5 = tables(high(w1), left)
            l4, l6 = tables(low(w1), left)
            l7, = tables(high(w2), left, False)
            for l, (co, si) in enumerate((l3, l4, l5, l6, l7)):
                cs5[(l, 0) + at] = co
                cs5[(l, 1) + at] = si
                ms5[(l,) + at] = kind_rows(w2, 3 + l)

    far = 1 - x1

    @pl.loop(0, 2)
    def _(i):
        gx0 = (x0 + i) % 2
        recv(b_aux.at[far, gx0], rb2.at[i])
        late_tables(far, gx0)
        for h in range(2):
            for hf in range(2):
                recv(b_co.at[far, gx0, :, :, zl0s[1 - h], hf], rb.at[i * 2 + h, hf])
            step_in_place(3, 2, {0: far, 1: gx0, 4: zl0s[1 - h]})
        step_in_place(4, 4, {0: far, 1: gx0})

    for b in range(2):
        step_in_place(5, 1, {0: far, 2: b})
    for b in range(2):
        step_in_place(6, 3, {0: far, 1: b})

    near = 1 - x0
    late_tables(x1, x0)
    step_in_place(3, 2, {0: x1, 1: x0})
    step_in_place(4, 4, {0: x1, 1: x0})
    recv(b_aux.at[x1, near], rb2.at[2])
    late_tables(x1, near)
    ev_w = ev[...]
    mine = x * 4 + nhs[0] * 2 + c
    for hf in range(2):
        for h in range(2):
            recv(b_co.at[x1, near, :, :, zl0s[1 - h], hf], rb.at[4 + h, hf])
            step_in_place(3, 2, {0: x1, 1: near, 4: zl0s[1 - h]}, hf)
        step_in_place(4, 4, {0: x1, 1: near}, hf)
        step_in_place(5, 1, {0: x1}, hf)
        step_in_place(6, 3, {0: x1}, hf)
        sums = [[o.reshape(2, 4, 2, 2, 16, 128).sum(axis=(1, 2)) for o in step(7, 0, {1: q}, hf)] for q in range(2)]
        if hf == 0:
            for q in range(2):
                for bit in range(2):
                    acc[bit, q] = sums[q][bit]
            continue
        total = jnp.concatenate([(sums[q][bit] + acc[bit, q]).reshape(64, 128) for bit in range(2) for q in range(2)], axis=0)
        big = total.astype(jnp.bfloat16)
        small = (total - big.astype(jnp.float32)).astype(jnp.bfloat16)
        r = (jnp.dot(big, ev_w, preferred_element_type=jnp.float32)
             + jnp.dot(small, ev_w, preferred_element_type=jnp.float32)).astype(jnp.bfloat16)
        osend[...] = r.reshape(2, 2, 2, 2, 16, 128)
        for dx in (2, 3, 1, 0):
            for dh in (1, 0):
                for dc in (0, 1):
                    to = (ns[0] % 4 * 4 + y, xs[dx] * 4 + zhs[dh] * 2 + cs[dc])
                    pltpu.make_async_remote_copy(
                        osend.at[xs[dx] // 2, xs[dx] % 2, zhs[dh], cs[dc]], out.at[mine], so, ro,
                        device_id=to, device_id_type=MESH).start()
    recv(b_aux.reshape(32, 3, 4, 128).at[pl.ds(0, 24)], sb2, True)
    recv(b_send.at[pl.ds(0, 6)], sb, True)
    recv(aux.at[pl.ds(0, 168)], sa.at[0], True)
    recv(a_co.at[pl.ds(0, 7)], sa.at[1], True)
    recv(aux.at[pl.ds(0, 56)], sq.at[0], True)
    recv(q_co.reshape(8, 4, 2, 16, 128).at[pl.ds(0, 7)], sq.at[1], True)
    recv(aux.at[pl.ds(0, 56)], sqa, True)
    recv(out, so, True)
    recv(out, ro)


def per_device(coefficients, phases, classes, blocks, evaluation):
    coef = coefficients.reshape(2, 2, 4, 4, 2, 2, 16, 128)
    wts = blocks.reshape(8, 512, 256)
    vmem = pl.BlockSpec(memory_space=pltpu.VMEM)
    hbm = pl.BlockSpec(memory_space=pltpu.HBM)
    bf, f32, i32 = jnp.bfloat16, jnp.float32, jnp.int32
    dma = pltpu.SemaphoreType.DMA
    result = pl.pallas_call(
        kernel,
        out_shape=pltpu.VMEM((16, 16, 128), bf),
        in_specs=[hbm] * 5,
        out_specs=vmem,
        scratch_shapes=[
            pltpu.VMEM((8, 64, 256), f32),
            pltpu.VMEM((8, 256), i32),
            pltpu.VMEM((128, 128), bf),
            pltpu.VMEM((8, 512, 256), bf),
            pltpu.VMEM((256, 3, 1, 128), i32),
            pltpu.VMEM((8, 8, 2, 2, 16, 128), bf),
            pltpu.VMEM((4, 2, 2, 2, 3, 8, 128), i32),
            pltpu.VMEM((4, 2, 2, 2, 3, 4, 128), i32),
            pltpu.VMEM((8, 4, 8, 16, 128), bf),
            pltpu.VMEM((2, 2, 2, 2, 2, 2, 4, 16, 128), bf),
            pltpu.VMEM((2, 2, 2, 2, 2, 3, 4, 128), i32),
            pltpu.VMEM((2, 2, 2, 4, 2, 16, 128), bf),
            pltpu.VMEM((2, 2, 2, 4, 2, 3, 1, 128), i32),
            pltpu.VMEM((2, 2, 2, 3, 8, 128), i32),
            pltpu.VMEM((3, 2, 4, 8, 128), f32),
            pltpu.VMEM((3, 4, 8, 128), f32),
            pltpu.VMEM((5, 2, 2, 2, 2, 2, 2, 8, 128), f32),
            pltpu.VMEM((5, 2, 2, 2, 2, 2, 8, 128), f32),
            pltpu.VMEM((2, 2, 2, 2, 16, 128), f32),
            pltpu.VMEM((2, 2, 2, 2, 16, 128), bf),
            dma((4,)), dma((10,)), dma((2,)), dma((8,)), dma((4,)),
            dma, dma((8, 2)), dma, dma((4,)), dma, dma, dma((4,)),
            pltpu.SemaphoreType.REGULAR, dma((2,)), dma((2,)), dma((2,)), dma, dma((2,)),
        ],
        compiler_params=pltpu.CompilerParams(
            collective_id=0, has_side_effects=True, vmem_limit_bytes=66912256),
    )(coef, phases.transpose(0, 2, 1), classes, wts, evaluation)
    return result[None]


def solution(mesh):
    placed = (
        P(("src", "tgt"), None, None),
        P(None, ("src", "tgt"), None),
        P(None, ("src", "tgt")),
        P(),
        P(),
    )
    return jax.shard_map(
        per_device, mesh=mesh, in_specs=placed,
        out_specs=P("tgt", "src", None, None), check_vma=False,
    )
```

```python
import jax
import jax.numpy as jnp
from jax import lax
from jax.experimental import pallas as pl
from jax.experimental.pallas import tpu as pltpu
from jax.sharding import PartitionSpec as P

MESH = pl.DeviceIdType.MESH
SIN = (3.141592502593994, -5.167698860168457, 2.5499982833862305, -0.59855055809021, 0.0807478204369545, -0.00608947454020381)
COS = (1.0, -4.93480110168457, 4.058694839477539, -1.3351584672927856, 0.23502980172634125, -0.025358984246850014, 0.0015939107397571206)
STEP = 10430.378350470453


def horner(coefs, v):
    acc = jnp.full_like(v, coefs[-1])
    for a in coefs[-2::-1]:
        acc = acc * v + a
    return acc


def sin_cos(k):
    u = k.astype(jnp.float32) * (1.0 / 32768.0)
    v = u * u
    return u * horner(SIN, v), horner(COS, v)


def high(w):
    return w >> 16


def low(w):
    return (w << 16) >> 16


def word(a, b):
    return (a << 16) | (b & 0xFFFF)


def tables(k, left, second=True):
    sine, cosine = sin_cos(k)
    sine_r, cosine_r = pltpu.roll(sine, 64, 1), pltpu.roll(cosine, 64, 1)
    out = [(jnp.where(left, cosine, cosine_r), jnp.where(left, -sine, sine_r))]
    if second:
        out.append((jnp.where(left, cosine_r, cosine), jnp.where(left, -sine_r, sine)))
    return out


def expand(rows):
    return jnp.broadcast_to(rows[..., None, :], rows.shape[:-1] + (16, 128))


def butterfly(x0, x1, m0, m1, weights, rot0, rot1):
    g, h = x0.shape[:2]
    shape, rows = (g, h, 16, 128), g * h * 16

    def split(x, m):
        one = x * expand(m).astype(jnp.bfloat16)
        return (x - one).reshape(rows, 128), one.reshape(rows, 128)

    a0, a1 = split(x0, m0)
    b0, b1 = split(x1, m1)
    s = jnp.dot(jnp.concatenate([a0, b0, a1, b1], axis=1), weights, preferred_element_type=jnp.float32)
    outs = []
    for half, (c, sn) in enumerate((rot0, rot1)):
        v = s[:, half * 128:(half + 1) * 128]
        outs.append((v.reshape(shape) * expand(c) + pltpu.roll(v, 64, 1).reshape(shape) * expand(sn)))
    return outs


def kernel(coef, ph_hbm, cls_hbm, wts_hbm, ev_hbm, out,
           ph, cls, ev, wts, aux, a_co, a_aux, p_send, b_send, b_co, b_aux, q_co, q_aux, qa, cs3, ms3, cs5, ms5, acc, osend,
           wsem, loc, sa, ra, ra2, sb, rb, sb2, rb2, so, ro, lb, known, sq, rq, rq2, sqa, rqa):
    copies = [pltpu.make_async_copy(a, b, wsem.at[i]) for i, (a, b) in enumerate(
        ((ph_hbm, ph), (cls_hbm, cls), (wts_hbm, wts), (ev_hbm, ev)))]
    for cp in copies:
        cp.start()
    s = lax.axis_index("src")
    t = lax.axis_index("tgt")
    y, zl = s % 4, s // 4
    c, zh, x = t % 2, (t // 2) % 2, t // 4
    x1, x0 = x // 2, x % 2
    ys = [(y + d) % 4 for d in range(4)]
    xs = [x, x1 * 2 + 1 - x0, (1 - x1) * 2 + x0, 3 - x]
    z = zh * 4 + zl
    zs = [(z + d) % 8 for d in range(8)]
    ns = [(z + d + 6) % 8 for d in range(8)]
    n1s, nhs = [v % 4 // 2 for v in ns], [v // 4 for v in ns]
    zl0s = [zl % 2, 1 - zl % 2]
    cs = [c, 1 - c]
    zhs = [zh, 1 - zh]
    me = (s, t)

    def dev(dx=0, dy=0, dz=0, dc=0):
        return zs[dz] % 4 * 4 + ys[dy], xs[dx] * 4 + zs[dz] // 4 * 2 + cs[dc]

    yc_peers = [(dy, dc) for dy in (2, 1, 3, 0) for dc in (0, 1) if (dy, dc) != (0, 0)]
    z_peers = (4, 3, 5, 2, 6, 1, 7)
    x_peers = (2, 1, 3)

    barrier = pltpu.get_barrier_semaphore()
    for dz in z_peers:
        pl.semaphore_signal(barrier, inc=1, device_id=dev(dz=dz), device_id_type=MESH)
    for dx in x_peers:
        pl.semaphore_signal(barrier, inc=1, device_id=dev(dx=dx), device_id_type=MESH)
    for dy, dc in yc_peers:
        pl.semaphore_signal(barrier, inc=1, device_id=dev(dy=dy, dc=dc), device_id_type=MESH)

    copies[0].wait()
    copies[1].wait()
    kinds = jnp.concatenate([cls[...], jnp.zeros((56, 256), jnp.int32)], axis=0)

    def fixed(l):
        return jnp.round(ph[l] * STEP).astype(jnp.int32)

    q = [fixed(l) for l in range(8)]
    aux[:, 0, 0, :] = jnp.concatenate([word(q[0], q[1]), word(q[2], kinds)], axis=0).T
    aux[:, 1, 0, :] = jnp.concatenate([word(q[3], q[4]), word(q[5], q[6])], axis=0).T
    aux[:, 2, 0, :] = jnp.concatenate([word(q[7], kinds), jnp.zeros((64, 256), jnp.int32)], axis=0).T
    aux_n = aux.reshape(2, 2, 4, 4, 2, 2, 3, 1, 128)

    pl.semaphore_wait(barrier, 17)
    for dx in x_peers:
        pl.semaphore_signal(known, inc=1, device_id=dev(dx=dx), device_id_type=MESH)

    def along_z(p):
        for dz in (3, 5, 1, 7) if p else (4, 2, 6, 0):
            at = (n1s[dz], zl0s[p], slice(None), x, nhs[dz], slice(None))
            for src, dst, ssem, rsem in ((aux_n, q_aux, sq.at[0], rq2.at[p]), (coef, q_co, sq.at[1], rq.at[p])):
                if dz == 0:
                    pltpu.make_async_copy(src.at[at], dst.at[p, zl // 2, zh], rsem).start()
                else:
                    pltpu.make_async_remote_copy(
                        src.at[at], dst.at[p, zl // 2, zh], ssem, rsem, device_id=dev(dz=dz), device_id_type=MESH).start()

    along_z(1)

    me_yc = y * 2 + c
    groups = (2, 3, 1)
    own_aux, own_co = [], {}

    for g, dx in enumerate(groups):
        for dy, dc in yc_peers:
            pltpu.make_async_remote_copy(
                aux_n.at[:, :, ys[dy], xs[dx], :, cs[dc]], a_aux.at[g, :, :, :, :, pl.ds(me_yc, 1)], sa.at[0], ra2.at[g],
                device_id=dev(dy=dy, dc=dc), device_id_type=MESH).start()
        own_aux.append(pltpu.make_async_copy(aux_n.at[:, :, y, xs[dx], :, c], a_aux.at[g, :, :, :, :, pl.ds(me_yc, 1)], lb.at[g]))
        own_aux[-1].start()
        for p in (1, 0):
            k = g * 2 + 1 - p
            for dy, dc in yc_peers:
                pltpu.make_async_remote_copy(
                    coef.at[:, zl0s[p], ys[dy], xs[dx], :, cs[dc]], a_co.at[k, me_yc], sa.at[1], ra.at[k],
                    device_id=dev(dy=dy, dc=dc), device_id_type=MESH).start()
            own_co[k] = pltpu.make_async_copy(coef.at[:, zl0s[p], y, xs[dx], :, c], a_co.at[k, me_yc], loc.at[k])
            own_co[k].start()
        if g == 0:
            along_z(0)
    copies[2].wait()
    copies[3].wait()

    def recv(ref, sem, send=False):
        cp = pltpu.make_async_remote_copy(ref, ref, sem, sem, device_id=me, device_id_type=MESH)
        if send:
            cp.wait_send()
        else:
            cp.wait_recv()

    me_slot = (x1, x0, zh, zl // 2, zl % 2)

    def pass_on(dx, dz, src, dst, ssem, rsem, half=()):
        if (dx, dz) == (0, 0):
            pltpu.make_async_copy(src, dst.at[me_slot + half], rsem).start()
        else:
            pltpu.make_async_remote_copy(
                src, dst.at[me_slot + half], ssem, rsem, device_id=dev(dx=dx, dz=dz), device_id_type=MESH).start()

    pl.semaphore_wait(known, 3)
    left = lax.broadcasted_iota(jnp.int32, (8, 128), 1) < 64

    def kind_rows(words, at):
        return jnp.broadcast_to(low(words)[:, at:at + 1], (8, 128)).astype(jnp.float32)

    def pack(w, v, ref, at):
        ref[at + (0,)] = w[:4]
        ref[at + (1,)] = w[4:]
        ref[at + (2,)] = jnp.where(left[:4], v[:4], pltpu.roll(v, 64, 1)[4:])

    def pass_chunk(k, dx, p, hf):
        for dz in (3, 5, 1, 7) if p else (4, 2, 6, 0):
            pass_on(dx, dz, b_send.at[k, n1s[dz] * 2 + nhs[dz], pl.ds(hf * 4, 4)], b_co, sb, rb.at[k, hf], (hf,))

    def early_levels(words, chunk):
        for n, w in enumerate(words):
            first, third = tables(high(w), left)
            second, = tables(low(w), left, False)
            for l, (co, si) in enumerate((first, second, third)):
                cs3[l, 0, n] = co
                cs3[l, 1, n] = si
                ms3[l, n] = kind_rows(w, 64 + l)
        cur = chunk()
        for l, bit in enumerate((1, 0, 2)):
            lows = [b for b in range(8) if not b & (1 << bit)]
            highs = [b + (1 << bit) for b in lows]

            def rows(table, chosen):
                return jnp.stack([table[:, b] for b in chosen], axis=0)

            def boxes(chosen):
                return jnp.stack([cur[b] for b in chosen], axis=0)

            co, si, mm = cs3[l, 0], cs3[l, 1], ms3[l]
            o0, o1 = butterfly(boxes(lows), boxes(highs), rows(mm, lows), rows(mm, highs), wts[l],
                               (rows(co, lows), rows(si, lows)), (rows(co, highs), rows(si, highs)))
            o0, o1 = o0.astype(jnp.bfloat16), o1.astype(jnp.bfloat16)
            for j in range(4):
                cur[lows[j]], cur[highs[j]] = o0[j], o1[j]
        return cur

    def chunk_of(k, own):
        def load():
            own.wait()
            recv(a_co.at[k, pl.ds(0, 7)], ra.at[k])
            return [a_co[k, b].reshape(4, 16, 128) for b in range(8)]
        return load

    own_qa, own_q = {}, {}
    for g, dx in enumerate(groups):
        own_aux[g].wait()
        recv(aux.at[pl.ds(0, 56)], ra2.at[g])
        for i in range(8):
            n1, n0, nh = i // 4, i // 2 % 2, i % 2
            pack(a_aux[g, n1, n0, nh, 1], a_aux[g, n1, n0, nh, 2], p_send, (g, n1, n0, nh))
        for dz in (4, 3, 5, 2, 6, 1, 7, 0):
            pass_on(dx, dz, p_send.at[g, n1s[dz], zl0s[dz % 2], nhs[dz]], b_aux, sb2, rb2.at[g])
        for p in (1, 0):
            k = g * 2 + 1 - p
            cur = early_levels([a_aux[g, n // 2, zl0s[p], n % 2, 0] for n in range(4)], chunk_of(k, own_co[k]))
            for b in range(8):
                b_send[k, :, b] = cur[b]
            pass_chunk(k, dx, p, 0)
            if g < 2:
                pass_chunk(k, dx, p, 1)
        if g < 2:
            q = 1 - g
            recv(q_aux.at[q], rq2.at[q])
            recv(q_co.at[q], rq.at[q])
            for dy, dc in yc_peers:
                to = dev(dy=dy, dc=dc)
                pltpu.make_async_remote_copy(
                    q_aux.at[q, :, :, ys[dy], cs[dc]], qa.at[q, :, :, :, pl.ds(me_yc, 1)], sqa, rqa.at[q],
                    device_id=to, device_id_type=MESH).start()
                pltpu.make_async_remote_copy(
                    q_co.at[q, :, :, ys[dy], cs[dc]], a_co.at[7 - q, me_yc], sa.at[1], ra.at[7 - q],
                    device_id=to, device_id_type=MESH).start()
            own_qa[q] = pltpu.make_async_copy(q_aux.at[q, :, :, y, c], qa.at[q, :, :, :, pl.ds(me_yc, 1)], loc.at[8 + q])
            own_qa[q].start()
            own_q[q] = pltpu.make_async_copy(q_co.at[q, :, :, y, c], a_co.at[7 - q, me_yc], loc.at[7 - q])
            own_q[q].start()

    pass_chunk(4, 1, 1, 1)
    pass_chunk(5, 1, 0, 1)
    for q in (1, 0):
        own_qa[q].wait()
        recv(aux.at[pl.ds(0, 28)], rqa.at[q])
        for i in range(4):
            pack(qa[q, i // 2, i % 2, 1], qa[q, i // 2, i % 2, 2], b_aux, (x1, x0, i % 2, i // 2, zl0s[q]))
        cur = early_levels([qa[q, n // 2, n % 2, 0] for n in range(4)], chunk_of(7 - q, own_q[q]))
        for n in range(4):
            for b in range(8):
                b_co[x1, x0, n % 2, n // 2, zl0s[q], b // 4, b % 4] = cur[b][n]

    def place(dim, bit, fixed_at):
        at = [slice(None)] * 5
        at[dim] = bit
        for d, v in fixed_at.items():
            at[d] = v
        return tuple(at)

    def step(l, dim, fixed_at, hf):
        height = 8 if hf is None else 4

        def boxes(bit):
            at = place(dim, bit, fixed_at)
            return b_co[at if hf is None else at + (hf,)].reshape(-1, height, 16, 128)

        def rows(ref, lead, bit):
            at = lead + place(dim, bit, fixed_at)
            return ref[at if hf is None else at + (pl.ds(hf * 4, 4),)].reshape(-1, height, 128)

        rots = [tuple(rows(cs5, (l - 3, i), bit) for i in range(2)) for bit in range(2)]
        return butterfly(boxes(0), boxes(1), rows(ms5, (l - 3,), 0), rows(ms5, (l - 3,), 1), wts[l], *rots)

    def step_in_place(l, dim, fixed_at, hf=None):
        for bit, o in enumerate(step(l, dim, fixed_at, hf)):
            at = place(dim, bit, fixed_at)
            lead = (2,) * (4 - len(fixed_at))
            if hf is None:
                b_co[at] = o.astype(jnp.bfloat16).reshape(lead + (2, 4, 16, 128))
            else:
                b_co[at + (hf,)] = o.astype(jnp.bfloat16).reshape(lead + (4, 16, 128))

    def late_tables(gx1, gx0):
        @pl.loop(0, 2)
        def _(z1):
          for j in range(4):
            at = (gx1, gx0, j // 2, z1, j % 2)
            w1 = jnp.concatenate([b_aux[at + (0,)], b_aux[at + (1,)]], axis=0)
            w2 = b_aux[at + (2,)]
            w2 = jnp.concatenate([w2, pltpu.roll(w2, 64, 1)], axis=0)
            l3, l5 = tables(high(w1), left)
            l4, l6 = tables(low(w1), left)
            l7, = tables(high(w2), left, False)
            for l, (co, si) in enumerate((l3, l4, l5, l6, l7)):
                cs5[(l, 0) + at] = co
                cs5[(l, 1) + at] = si
                ms5[(l,) + at] = kind_rows(w2, 3 + l)

    far = 1 - x1

    @pl.loop(0, 2)
    def _(i):
        gx0 = (x0 + i) % 2
        recv(b_aux.at[far, gx0], rb2.at[i])
        late_tables(far, gx0)
        for h in range(2):
            for hf in range(2):
                recv(b_co.at[far, gx0, :, :, zl0s[1 - h], hf], rb.at[i * 2 + h, hf])
            step_in_place(3, 2, {0: far, 1: gx0, 4: zl0s[1 - h]})
        step_in_place(4, 4, {0: far, 1: gx0})

    for b in range(2):
        step_in_place(5, 1, {0: far, 2: b})
    for b in range(2):
        step_in_place(6, 3, {0: far, 1: b})

    near = 1 - x0
    late_tables(x1, x0)
    step_in_place(3, 2, {0: x1, 1: x0})
    step_in_place(4, 4, {0: x1, 1: x0})
    recv(b_aux.at[x1, near], rb2.at[2])
    late_tables(x1, near)
    ev_w = ev[...]
    mine = x * 4 + nhs[0] * 2 + c
    for hf in range(2):
        for h in range(2):
            recv(b_co.at[x1, near, :, :, zl0s[1 - h], hf], rb.at[4 + h, hf])
            step_in_place(3, 2, {0: x1, 1: near, 4: zl0s[1 - h]}, hf)
        step_in_place(4, 4, {0: x1, 1: near}, hf)
        step_in_place(5, 1, {0: x1}, hf)
        step_in_place(6, 3, {0: x1}, hf)
        sums = [[o.reshape(2, 4, 2, 2, 16, 128).sum(axis=(1, 2)) for o in step(7, 0, {1: q}, hf)] for q in range(2)]
        if hf == 0:
            for q in range(2):
                for bit in range(2):
                    acc[bit, q] = sums[q][bit]
            continue
        total = jnp.concatenate([(sums[q][bit] + acc[bit, q]).reshape(64, 128) for bit in range(2) for q in range(2)], axis=0)
        big = total.astype(jnp.bfloat16)
        small = (total - big.astype(jnp.float32)).astype(jnp.bfloat16)
        r = (jnp.dot(big, ev_w, preferred_element_type=jnp.float32)
             + jnp.dot(small, ev_w, preferred_element_type=jnp.float32)).astype(jnp.bfloat16)
        osend[...] = r.reshape(2, 2, 2, 2, 16, 128)
        for dx in (2, 3, 1, 0):
            for dh in (1, 0):
                for dc in (0, 1):
                    to = (ns[0] % 4 * 4 + y, xs[dx] * 4 + zhs[dh] * 2 + cs[dc])
                    pltpu.make_async_remote_copy(
                        osend.at[xs[dx] // 2, xs[dx] % 2, zhs[dh], cs[dc]], out.at[mine], so, ro,
                        device_id=to, device_id_type=MESH).start()
    recv(b_aux.reshape(32, 3, 4, 128).at[pl.ds(0, 24)], sb2, True)
    recv(b_send.at[pl.ds(0, 6)], sb, True)
    recv(aux.at[pl.ds(0, 168)], sa.at[0], True)
    recv(a_co.at[pl.ds(0, 7)], sa.at[1], True)
    recv(aux.at[pl.ds(0, 56)], sq.at[0], True)
    recv(q_co.reshape(8, 4, 2, 16, 128).at[pl.ds(0, 7)], sq.at[1], True)
    recv(aux.at[pl.ds(0, 56)], sqa, True)
    recv(out, so, True)
    recv(out, ro)


def per_device(coefficients, phases, classes, blocks, evaluation):
    coef = coefficients.reshape(2, 2, 4, 4, 2, 2, 16, 128)
    wts = blocks.reshape(8, 512, 256)
    vmem = pl.BlockSpec(memory_space=pltpu.VMEM)
    hbm = pl.BlockSpec(memory_space=pltpu.HBM)
    bf, f32, i32 = jnp.bfloat16, jnp.float32, jnp.int32
    dma = pltpu.SemaphoreType.DMA
    result = pl.pallas_call(
        kernel,
        out_shape=pltpu.VMEM((16, 16, 128), bf),
        in_specs=[hbm] * 5,
        out_specs=vmem,
        scratch_shapes=[
            pltpu.VMEM((8, 64, 256), f32),
            pltpu.VMEM((8, 256), i32),
            pltpu.VMEM((128, 128), bf),
            pltpu.VMEM((8, 512, 256), bf),
            pltpu.VMEM((256, 3, 1, 128), i32),
            pltpu.VMEM((8, 8, 2, 2, 16, 128), bf),
            pltpu.VMEM((4, 2, 2, 2, 3, 8, 128), i32),
            pltpu.VMEM((4, 2, 2, 2, 3, 4, 128), i32),
            pltpu.VMEM((8, 4, 8, 16, 128), bf),
            pltpu.VMEM((2, 2, 2, 2, 2, 2, 4, 16, 128), bf),
            pltpu.VMEM((2, 2, 2, 2, 2, 3, 4, 128), i32),
            pltpu.VMEM((2, 2, 2, 4, 2, 16, 128), bf),
            pltpu.VMEM((2, 2, 2, 4, 2, 3, 1, 128), i32),
            pltpu.VMEM((2, 2, 2, 3, 8, 128), i32),
            pltpu.VMEM((3, 2, 4, 8, 128), f32),
            pltpu.VMEM((3, 4, 8, 128), f32),
            pltpu.VMEM((5, 2, 2, 2, 2, 2, 2, 8, 128), f32),
            pltpu.VMEM((5, 2, 2, 2, 2, 2, 8, 128), f32),
            pltpu.VMEM((2, 2, 2, 2, 16, 128), f32),
            pltpu.VMEM((2, 2, 2, 2, 16, 128), bf),
            dma((4,)), dma((10,)), dma((2,)), dma((8,)), dma((4,)),
            dma, dma((8, 2)), dma, dma((4,)), dma, dma, dma((4,)),
            pltpu.SemaphoreType.REGULAR, dma((2,)), dma((2,)), dma((2,)), dma, dma((2,)),
        ],
        compiler_params=pltpu.CompilerParams(
            collective_id=0, has_side_effects=True, vmem_limit_bytes=66912256),
    )(coef, phases.transpose(0, 2, 1), classes, wts, evaluation)
    return result[None]


def solution(mesh):
    placed = (
        P(("src", "tgt"), None, None),
        P(None, ("src", "tgt"), None),
        P(None, ("src", "tgt")),
        P(),
        P(),
    )
    return jax.shard_map(
        per_device, mesh=mesh, in_specs=placed,
        out_specs=P("tgt", "src", None, None), check_vma=False,
    )
```
